256 devices in a mesh: role: 2 (over core), dp: 32 (over x, z), mp: 4 (over y).
Axes of the slice: x: 4, y: 4, z: 8, core: 2. Of those that a mesh axis runs over, the one named last changes fastest.
Arguments:
- noise: bfloat16 [4096, 3072], P('dp', 'mp'), may hold values from -6 to 6
- gen_gain: float32 [3072], replicated, may hold values from 0.25 to 1.75
- gen_weight: bfloat16 [3072, 3072], P('dp', 'mp'), may hold values from -0.109375 to 0.109375
- routes: int32 [1024, 1], replicated, may hold values from 0 to 31; in each aligned block of 32 rows (0 to 31, 32 to 63, ...) at most 2 rows name the same one
- critic_noise: bfloat16 [8192, 3072], P('dp', 'mp'), may hold values from -6 to 6
- critic_steps: int32 [2048], P('dp'), may hold values from 20 to 979
- crit_mod: float32 [2, 2, 3072], P('role'), may hold values from -3 to 3
- crit_first: bfloat16 [2, 3072, 3072], P('role', 'dp', 'mp'), may hold values from -0.109375 to 0.109375
- crit_second: bfloat16 [2, 3072, 3072], P('role', 'dp', 'mp'), may hold values from -0.109375 to 0.109375
Outputs:
- noise_grad: float32 [4096, 4, 2, 384], P('dp', 'mp', 'role')
- grad_first: float32 [2, 3072, 3072], P('role', 'dp', 'mp')
- grad_second: float32 [2, 3072, 3072], P('role', 'dp', 'mp')
The draws below stay inside these ranges and needn't reach their ends.
Inputs may be any that keep to these rules, and one draw needn't show every extreme that they name: `routes`: within the 32 rows of one index of dp, no value appears more than 2 times, and in every draw some value appears exactly 2 times in some such block.
All inputs are finite; a program needn't handle non-finite values.
Results may differ from the reference program's by a relative error of at most 0.01.
Values may be sent and summed in bfloat16 or wider, within the bound.
A program may use at most 128 MiB of HBM per device.

```python
import math
import jax
import jax.numpy as jnp
import numpy as np
from jax import lax

D = 3072
TOK_DEV = 128
BT = 4
NB = 32
MOST = 2
TOKENS = 4096
BLOCKS = 1024
CTOK = 8192
CBLOCKS = 2048
HALFW = 384
N_DP = 32
N_MP = 4


def plant(values, stream_key, smallest, largest):
    spot = [jax.random.randint(jax.random.fold_in(stream_key, axis), (), 0, length) for axis, length in enumerate(values.shape)]
    widest = values.shape.index(max(values.shape))
    next_to = spot[:widest] + [(spot[widest] + 1) % values.shape[widest]] + spot[widest + 1:]
    return values.at[tuple(spot)].set(smallest).at[tuple(next_to)].set(largest)


def level_of(rng, extent, split, smallest, largest):
    def one(position, parts):
        steps = jax.random.uniform(jax.random.fold_in(jax.random.fold_in(rng, 6), position), (parts,), jnp.float32, smallest / len(split), largest / len(split))
        return jnp.repeat(jnp.exp(steps), extent[position] // parts).reshape((-1,) + (1,) * (len(extent) - position - 1))

    factor_of = one(*split[0])
    for cut in split[1:]:
        factor_of = factor_of * one(*cut)
    return factor_of


def deal_out(stream_key, own, number, rows, number_of, top, limit, skew):
    order = jax.random.permutation(stream_key, number_of)
    heavy_load, ordinary = shares(number_of, rows * top, limit, skew, True), shares(number_of, rows * top, limit, skew, False)
    places = jnp.arange(number_of)

    def named(tallies, turn):
        used = int((tallies > 0).sum())
        fixed = max(1, used // 4)
        passed = fixed + (places - fixed + turn * (used - fixed)) % max(1, number_of - fixed)
        return jnp.zeros((number_of,), jnp.int32).at[order[jnp.where(places < fixed, places, passed)]].set(jnp.asarray(tallies, jnp.int32))

    tallies = jnp.where(number % 4 == 0, named(heavy_load, number // 4), named(ordinary, number - number // 4 - 1))
    mixed = jax.random.permutation(jax.random.fold_in(own, 3), number_of)
    source_of, sink = mixed[0:number_of // 2 * 2:2], mixed[1:number_of // 2 * 2:2]
    room = jnp.minimum(tallies[source_of] - 1, limit - tallies[sink]) // 2
    room = jnp.where((source_of == order[0]) | (sink == order[0]) | (tallies[sink] == 0), 0, jnp.maximum(room, 0))
    passed = jax.random.randint(jax.random.fold_in(own, 4), (number_of // 2,), 0, 1 << 20) % (room + 1)
    tallies = tallies.at[source_of].add(-passed).at[sink].add(passed)
    items = jnp.searchsorted(jnp.cumsum(tallies), jnp.arange(rows * top), side="right").astype(jnp.int32)
    table = items.reshape(top, rows).T
    table = table[jax.random.permutation(jax.random.fold_in(own, 1), rows)]
    turn = jax.random.randint(jax.random.fold_in(own, 2), (rows, 1), 0, top)
    return jnp.take_along_axis(table, (jnp.arange(top)[None, :] + turn) % top, axis=1)


def shares(number_of, total, limit, lean, full):
    portions = [(1 << 20) // math.isqrt(standing ** lean) + 1 for standing in range(1, number_of + 1)]
    largest = limit if full else min(limit, max(-(-total // number_of), total * portions[0] // sum(portions)))
    least = 1 if total - largest >= number_of - 1 else 0
    holding, spare = [largest] + [least] * (number_of - 1), total - largest - least * (number_of - 1)
    while spare > 0:
        free = [i for i in range(1, number_of) if holding[i] < largest] or [i for i in range(1, number_of) if holding[i] < limit]
        whole, remaining = sum([portions[i] for i in free]), spare
        for i in free:
            extra = min(limit - holding[i], max(1, remaining * portions[i] // whole), spare)
            holding[i] = holding[i] + extra
            spare = spare - extra
    return np.array(holding)


def scatter_about(stream_key, extent, deviation, bound, split=(), held_as=jnp.bfloat16):
    result = jax.random.normal(stream_key, extent, jnp.float32) * deviation
    if len(split) > 0:
        result = level_of(stream_key, extent, split, -0.22, 0.18) * result
    return jnp.clip(result, min=-bound, max=bound).astype(held_as)


def setup_inputs(seed: int = 0) -> dict:
    arg_keys = jax.random.split(jax.random.key(seed), 10)
    noise = scatter_about(arg_keys[0], (TOKENS, D), 1.0, 6.0, ((0, 32), (1, 4)))
    gen_gain = jnp.clip(1.0 + 0.15 * jax.random.normal(arg_keys[1], (D,), jnp.float32), 0.25, 1.75)
    gen_weight = scatter_about(arg_keys[2], (D, D), D ** -0.5, 0.109375, ((0, 32), (1, 4)))
    routes_keys = jax.random.split(jax.random.fold_in(arg_keys[3], 1), BLOCKS // NB)
    routes_turns = jax.random.permutation(jax.random.fold_in(arg_keys[3], 3), BLOCKS // NB)
    routes = jax.vmap(lambda own, number: deal_out(jax.random.fold_in(arg_keys[3], 2), own, number, NB, N_DP, 1, MOST, 2))(routes_keys, routes_turns).reshape((BLOCKS, 1))
    critic_noise = scatter_about(arg_keys[4], (CTOK, D), 1.0, 6.0, ((0, 32), (1, 4)))
    critic_steps = plant(jax.random.randint(arg_keys[5], (CBLOCKS,), 20, 980), jax.random.fold_in(arg_keys[5], 1), 20, 979).astype(jnp.int32)
    crit_mod = scatter_about(arg_keys[6], (2, 2, D), 1.0, 3.0, ((0, 2),), jnp.float32)
    crit_first = scatter_about(arg_keys[7], (2, D, D), D ** -0.5, 0.109375, ((0, 2), (1, 32), (2, 4)))
    crit_second = scatter_about(arg_keys[8], (2, D, D), D ** -0.5, 0.109375, ((0, 2), (1, 32), (2, 4)))
    return {"noise": noise, "gen_gain": gen_gain, "gen_weight": gen_weight, "routes": routes, "critic_noise": critic_noise, "critic_steps": critic_steps, "crit_mod": crit_mod, "crit_first": crit_first, "crit_second": crit_second}


epsilon = 1e-06
levels = 1000.0

def norm_act(field, scale):
    root = lax.rsqrt(lax.optimization_barrier(jnp.mean(field * field, axis=-1, keepdims=True)) + epsilon)
    normed = field * root
    shaped = normed * scale
    return (jax.nn.silu(shaped).astype(jnp.bfloat16), normed, shaped, root)

def slope(shaped):
    sigma = jax.nn.sigmoid(shaped)
    return sigma * (1.0 + shaped * (1.0 - sigma))

def norm_back(grad_act, normed, shaped, root, scale):
    grad_norm = grad_act * slope(shaped) * scale
    return root * (grad_norm - normed * lax.optimization_barrier(jnp.mean(grad_norm * normed, axis=-1, keepdims=True)))

def rounded(value):
    return lax.optimization_barrier(value.astype(jnp.bfloat16)).astype(jnp.float32)

def column_sum(left, weight):
    width = D // N_MP
    total = jnp.zeros((left.shape[0], D), jnp.float32)
    for block in range(N_MP):
        piece = jnp.dot(left[:, block * width:(block + 1) * width], weight[:, block * width:(block + 1) * width].T, preferred_element_type=jnp.float32)
        total = total + rounded(piece)
    return total

def group_sum(left, right):
    count = left.shape[0] // N_DP

    def step(total, group):
        start = (group * count).astype(jnp.int32)
        part_left = lax.dynamic_slice_in_dim(left, start, count, 0)
        part_right = lax.dynamic_slice_in_dim(right, start, count, 0)
        term = lax.dot_general(part_left, part_right, (((0,), (0,)), ((), ())), preferred_element_type=jnp.float32)
        return (total + rounded(term), None)
    total, _ = lax.scan(step, jnp.zeros((D, D), jnp.float32), jnp.arange(N_DP, dtype=jnp.int32))
    return total

def reference(noise, gen_gain, gen_weight, routes, critic_noise, critic_steps, crit_mod, crit_first, crit_second):
    gen_act, gen_normed, gen_shaped, gen_root = norm_act(noise.astype(jnp.float32), gen_gain[None, :])
    generated = (noise.astype(jnp.float32) + jnp.dot(gen_act, gen_weight, preferred_element_type=jnp.float32)).astype(jnp.bfloat16)
    target_index = routes[:, 0].astype(jnp.int32)
    index = jnp.arange(BLOCKS, dtype=jnp.int32)
    source = index // NB
    earlier = (target_index[:, None] == target_index[None, :]) & (source[:, None] == source[None, :]) & (index[None, :] < index[:, None])
    rank = lax.optimization_barrier(jnp.sum(earlier.astype(jnp.int32), axis=1)).astype(jnp.int32)
    slot = (target_index * (N_DP * MOST) + source * MOST + rank).astype(jnp.int32)
    clean = jnp.zeros((CBLOCKS, BT, D), jnp.bfloat16).at[slot].set(generated.reshape(BLOCKS, BT, D)).reshape(CTOK, D)
    valid = jnp.repeat(jnp.zeros((CBLOCKS,), jnp.float32).at[slot].set(1.0), BT)[:, None]
    level = jnp.repeat(critic_steps.astype(jnp.float32) / levels, BT)[:, None]
    clean_f = clean.astype(jnp.float32)
    noise_f = critic_noise.astype(jnp.float32)
    noisy = ((1.0 - level) * clean_f + level * noise_f).astype(jnp.bfloat16)
    target = noise_f - clean_f
    preds = []
    firsts = []
    seconds = []
    for network in range(2):
        scale_one = 1.0 + level * crit_mod[network, 0][None, :]
        scale_two = 1.0 + level * crit_mod[network, 1][None, :]
        first, _, _, _ = norm_act(noisy.astype(jnp.float32), scale_one)
        hidden = (noisy.astype(jnp.float32) + jnp.dot(first, crit_first[network], preferred_element_type=jnp.float32)).astype(jnp.bfloat16)
        second, normed, shaped, root = norm_act(hidden.astype(jnp.float32), scale_two)
        pred = (hidden.astype(jnp.float32) + jnp.dot(second, crit_second[network], preferred_element_type=jnp.float32)).astype(jnp.bfloat16)
        delta = ((pred.astype(jnp.float32) - target) * valid / TOK_DEV).astype(jnp.bfloat16)
        seconds.append(group_sum(second, delta))
        carried = column_sum(delta, crit_second[network])
        upstream = (delta.astype(jnp.float32) + norm_back(carried, normed, shaped, root, scale_two)).astype(jnp.bfloat16)
        firsts.append(group_sum(first, upstream))
        preds.append(pred)
    gap = (1.0 - level) * (preds[1].astype(jnp.float32) - preds[0].astype(jnp.float32))
    back_blocks = gap.astype(jnp.bfloat16).reshape(CBLOCKS, BT, D)[slot]
    returned = back_blocks.reshape(TOKENS, D)
    carried_gen = column_sum(returned, gen_weight)
    noise_grad = returned.astype(jnp.float32) + norm_back(carried_gen, gen_normed, gen_shaped, gen_root, gen_gain[None, :])
    return (noise_grad.reshape(TOKENS, N_MP, 2, HALFW), jnp.stack(firsts), jnp.stack(seconds))
```

```python
import jax
import jax.numpy as jnp
from jax import lax
from jax.sharding import Mesh
from jax.sharding import PartitionSpec as P

D = 3072
TOK_DEV = 128
BT = 4
R, X, Z, Y = "role", "dp_0", "dp_1", "mp"
DP = (X, Z)
YZ = (Y, Z)
F32, BF16 = jnp.float32, jnp.bfloat16

epsilon = 1e-06
levels = 1000.0


def copy_for_each(shard, axis):
    length = lax.axis_size(axis)
    return lax.all_to_all(
        jnp.broadcast_to(shard[None], (length, *shard.shape)), axis, 0, 0, tiled=True
    )


def collect_rows(shard, axis):
    return copy_for_each(shard, axis).reshape(-1, *shard.shape[1:])


def summed_rows_of(term, axis):
    length = lax.axis_size(axis)
    pieces = term.astype(BF16).reshape(length, -1, term.shape[-1])
    pieces = lax.all_to_all(pieces, axis, 0, 0, tiled=True)
    return jnp.sum(pieces.astype(F32), axis=0)


def of_everyone(value, axis):
    return copy_for_each(value, axis).sum(axis=0)


def swapped(block):
    count = lax.axis_size(X)
    route = [(a * count + b, b * count + a) for a in range(count) for b in range(count)]
    return lax.ppermute(block, (X, Y), route)


def partner(block):
    return lax.ppermute(block, R, [(0, 1), (1, 0)])


def root_of(block, axis):
    block = block.astype(F32)
    total = of_everyone(jnp.sum(block * block, axis=-1)[None], axis)[0]
    return lax.rsqrt(total / D + epsilon)[:, None]


def shaped_of(block, root, scale):
    normed = block.astype(F32) * root
    return normed, normed * scale


def act(block, root, scale):
    return jax.nn.silu(shaped_of(block, root, scale)[1]).astype(BF16)


def slope(shaped):
    sigma = jax.nn.sigmoid(shaped)
    return sigma * (1.0 + shaped * (1.0 - sigma))


def mm(left, right, a, b):
    return lax.dot_general(
        left, right, (((a,), (b,)), ((), ())), preferred_element_type=F32
    )


def columns_of(array, index, width):
    return lax.dynamic_slice_in_dim(array, index * width, width, array.ndim - 1)


def shards(
    noise,
    gen_gain,
    gen_weight,
    routes,
    critic_noise,
    critic_steps,
    crit_mod,
    crit_first,
    crit_second,
):
    width = noise.shape[1]
    groups = lax.axis_size(DP)
    x, y, z, role = (lax.axis_index(a) for a in (X, Y, Z, R))
    blocks_here = noise.shape[0] // BT
    most = 2 * blocks_here // groups

    gen_full = lax.all_gather(swapped(gen_weight), Z, axis=0, tiled=True)
    first_full = lax.all_gather(crit_first[0], Z, axis=0, tiled=True)
    second_full = lax.all_gather(swapped(crit_second[0]), Z, axis=0, tiled=True)

    noise_q = swapped(noise)
    crit_noise_q = swapped(critic_noise)
    steps_all = collect_rows(critic_steps, X)
    level_all = jnp.repeat(steps_all.astype(F32) / levels, BT)[:, None]
    rows = critic_noise.shape[0]
    level_p = lax.dynamic_slice_in_dim(level_all, x * rows, rows, 0)
    level_q = lax.dynamic_slice_in_dim(level_all, y * rows, rows, 0)
    modulation = crit_mod[0]
    mod_one = columns_of(modulation[0], x, width)[None, :]
    mod_two = columns_of(modulation[1], y, width)[None, :]
    gain_y = columns_of(gen_gain, y, width)[None, :]

    gen_root = root_of(noise, Y)
    gen_root_all = collect_rows(gen_root[:, 0], X)[:, None]
    gen_act = act(collect_rows(noise, X), gen_root_all, gain_y)
    generated = (noise_q.astype(F32) + summed_rows_of(mm(gen_act, gen_full, 1, 0), Y)).astype(BF16)

    me_index = y * lax.axis_size(Z) + z
    table = routes[:, 0]
    target_index = lax.dynamic_slice_in_dim(table, me_index * blocks_here, blocks_here, 0)
    order = jnp.arange(blocks_here, dtype=jnp.int32)
    earlier = (target_index[:, None] == target_index[None, :]) & (order[None, :] < order[:, None])
    rank = jnp.sum(earlier.astype(jnp.int32), axis=1)
    slot_here = target_index * most + rank
    placing = (jnp.arange(groups * most, dtype=jnp.int32)[:, None] == slot_here[None, :]).astype(
        BF16
    )
    outgoing = jnp.dot(
        placing, generated.reshape(blocks_here, BT * width), preferred_element_type=F32
    )
    outgoing = outgoing.astype(BF16).reshape(groups, most * BT, width)
    incoming = lax.all_to_all(outgoing, YZ, split_axis=0, concat_axis=0, tiled=True)
    clean = incoming.reshape(groups * most * BT, width)
    counts = jnp.sum((table.reshape(groups, blocks_here) == me_index).astype(jnp.int32), axis=1)
    filled = (jnp.arange(most, dtype=jnp.int32)[None, :] < counts[:, None]).astype(F32)
    valid = jnp.repeat(filled.reshape(groups * most), BT)[:, None]

    clean_f = clean.astype(F32)
    crit_noise_f = crit_noise_q.astype(F32)
    noisy = ((1.0 - level_q) * clean_f + level_q * crit_noise_f).astype(BF16)
    target = crit_noise_f - clean_f

    noisy_root = collect_rows(root_of(noisy, X)[:, 0], Y)[:, None]
    first = act(collect_rows(noisy, Y), noisy_root, 1.0 + level_all * mod_one)
    hidden = (
        swapped(noisy).astype(F32) + summed_rows_of(mm(first, first_full, 1, 0), X)
    ).astype(BF16)

    hidden_root = root_of(hidden, Y)
    root_all = collect_rows(hidden_root[:, 0], X)[:, None]
    second = act(collect_rows(hidden, X), root_all, 1.0 + level_all * mod_two)
    pred = (
        swapped(hidden).astype(F32) + summed_rows_of(mm(second, second_full, 1, 0), Y)
    ).astype(BF16)
    pred_f = pred.astype(F32)
    delta = ((pred_f - target) * valid / TOK_DEV).astype(BF16)

    delta_all = collect_rows(delta, Y)
    owned = summed_rows_of(mm(delta_all, second_full, 1, 1), X)
    term_two = mm(second, delta_all, 0, 0).astype(BF16)
    grad_two = swapped(lax.psum_scatter(term_two, Z, scatter_dimension=0, tiled=True)).astype(F32)

    scale_two = 1.0 + level_p * mod_two
    normed, shaped = shaped_of(hidden, hidden_root, scale_two)
    grad_norm = owned * slope(shaped) * scale_two
    inner = of_everyone(jnp.sum(grad_norm * normed, axis=-1)[None], Y)[0][:, None]
    back = hidden_root * (grad_norm - normed * (inner / D))
    upstream = (swapped(delta).astype(F32) + back).astype(BF16)
    term_one = mm(first, collect_rows(upstream, X), 0, 0).astype(BF16)
    grad_one = lax.psum_scatter(term_one, Z, scatter_dimension=0, tiled=True).astype(F32)

    other_f = partner(pred).astype(F32)
    difference = jnp.where(role == 1, pred_f - other_f, other_f - pred_f)
    gap = ((1.0 - level_q) * difference).astype(BF16).reshape(groups, most * BT, width)
    coming_back = lax.all_to_all(gap, YZ, split_axis=0, concat_axis=0, tiled=True)
    picked = mm(placing, coming_back.reshape(groups * most, BT * width), 0, 0)
    returned = picked.astype(BF16).reshape(blocks_here * BT, width)

    half = width // 2
    mine = lambda array: columns_of(array, role, half)
    weight_half = lax.dynamic_slice_in_dim(gen_full, role * half, half, 0)
    gen_owned = summed_rows_of(mm(collect_rows(returned, Y), weight_half, 1, 1), X)
    normed, shaped = shaped_of(mine(noise), gen_root, mine(gain_y))
    grad_norm = gen_owned * slope(shaped) * mine(gain_y)
    inner = of_everyone(jnp.sum(grad_norm * normed, axis=-1)[None], (R, Y))[0][:, None]
    back = gen_root * (grad_norm - normed * (inner / D))
    noise_grad = mine(swapped(returned)).astype(F32) + back
    return (noise_grad.reshape(-1, 1, 1, half), grad_one[None], grad_two[None])


def solution(mesh):
    split = Mesh(
        mesh.devices.reshape(mesh.shape[R], 4, mesh.shape["dp"] // 4, mesh.shape[Y]),
        (R, X, Z, Y),
    )
    in_specs = (
        P(DP, Y),
        P(),
        P(DP, Y),
        P(),
        P(DP, Y),
        P(DP),
        P(R, None, None),
        P(R, DP, Y),
        P(R, DP, Y),
    )
    out_specs = (P(DP, Y, R, None), P(R, DP, Y), P(R, DP, Y))
    return jax.shard_map(
        shards, mesh=split, in_specs=in_specs, out_specs=out_specs, check_vma=False
    )
```

```python
import functools

import jax
import jax.numpy as jnp
from jax import lax
from jax.experimental import pallas as pl
from jax.experimental.pallas import tpu as pltpu
from jax.sharding import Mesh
from jax.sharding import PartitionSpec as P

D = 3072
TOK_DEV = 128
BT = 4
R, X, Z, Y = "role", "dp_0", "dp_1", "mp"
DP = (X, Z)
YZ = (Y, Z)
F32, BF16 = jnp.float32, jnp.bfloat16

epsilon = 1e-06
levels = 1000.0


def copy_for_each(shard, axis):
    length = lax.axis_size(axis)
    return lax.all_to_all(
        jnp.broadcast_to(shard[None], (length, *shard.shape)), axis, 0, 0, tiled=True
    )


def collect_rows(shard, axis):
    return copy_for_each(shard, axis).reshape(-1, *shard.shape[1:])


def summed_rows_of(term, axis):
    length = lax.axis_size(axis)
    pieces = term.astype(BF16).reshape(length, -1, term.shape[-1])
    pieces = lax.all_to_all(pieces, axis, 0, 0, tiled=True)
    return jnp.sum(pieces.astype(F32), axis=0)


def of_everyone(value, axis):
    return copy_for_each(value, axis).sum(axis=0)


def swapped(block):
    count = lax.axis_size(X)
    route = [(a * count + b, b * count + a) for a in range(count) for b in range(count)]
    return lax.ppermute(block, (X, Y), route)


def partner(block):
    return lax.ppermute(block, R, [(0, 1), (1, 0)])


def root_of(block, axis):
    block = block.astype(F32)
    total = of_everyone(jnp.sum(block * block, axis=-1)[None], axis)[0]
    return lax.rsqrt(total / D + epsilon)[:, None]


def shaped_of(block, root, scale):
    normed = block.astype(F32) * root
    return normed, normed * scale


def act(block, root, scale):
    return jax.nn.silu(shaped_of(block, root, scale)[1]).astype(BF16)


def slope(shaped):
    sigma = jax.nn.sigmoid(shaped)
    return sigma * (1.0 + shaped * (1.0 - sigma))


def mm(left, right, a, b):
    return lax.dot_general(
        left, right, (((a,), (b,)), ((), ())), preferred_element_type=F32
    )


def columns_of(array, index, width):
    return lax.dynamic_slice_in_dim(array, index * width, width, array.ndim - 1)


H = 2
STEP = 32
MESH = pl.DeviceIdType.MESH


def sigmoid(v):
    return 1.0 / (1.0 + jnp.exp(-v))


def critic_kernel(
    n,
    nz,
    clean,
    cnoise,
    level,
    valid,
    mod_one,
    mod_two,
    w1_shard,
    w2_shard,
    gap,
    grad_one,
    grad_two,
    w1,
    w2,
    noisy_all,
    first_all,
    hidden_all,
    second_all,
    delta_all,
    up_all,
    root_q,
    root_p,
    hidden,
    pred,
    pred_other,
    swap_buf,
    part_out,
    part_in,
    own,
    g1_out,
    g1_in,
    g2_out,
    g2_in,
    column,
    stat_out,
    stat_in,
    inner_out,
    inner_in,
    w_sem,
    ag_sem,
    rs_sem,
    swap_sem,
    stat_sem,
    inner_sem,
    g_sem,
    role_sem,
):
    r, x, z, y = (lax.axis_index(a) for a in (R, X, Z, Y))
    rows, width = clean.shape
    hr = rows // H
    wr = w1_shard.shape[0]
    lanes = width // 128
    group = n * n
    here = x * n + y

    def dev(role=r, at_x=x, at_z=z, at_y=y):
        return (role, at_x, at_z, at_y)

    def remote(src, dst, sems, index, to):
        return pltpu.make_async_remote_copy(
            src_ref=src,
            dst_ref=dst,
            send_sem=sems.at[(0, *index)],
            recv_sem=sems.at[(1, *index)],
            device_id=to,
            device_id_type=MESH,
        )

    sent = []

    def each(low, high, body):
        def step(k, carry):
            body(k)
            return carry

        lax.fori_loop(low, high, step, 0)

    def wide(narrow):
        return jnp.concatenate([narrow] * lanes, axis=1)

    def cut(ref, start, count):
        return ref.at[pl.ds(pl.multiple_of(start, 16), count), :]

    barrier = pltpu.get_barrier_semaphore()

    def greet(to):
        pl.semaphore_signal(barrier, inc=1, device_id=to, device_id_type=MESH)

    def at(index):
        index = lax.rem(index, group)
        return index // n, lax.rem(index, n)

    def greet_plane(k):
        ax, ay = at(here + k)
        greet(dev(at_x=ax, at_y=ay))

    def greet_z(k):
        az = lax.rem(z + k, nz)
        greet(dev(at_z=az))
        greet(dev(at_x=y, at_z=az, at_y=x))

    each(1, group, greet_plane)
    each(1, nz, greet_z)
    greet(dev(role=1 - r))
    pl.semaphore_wait(barrier, group - 1 + 2 * (nz - 1) + 1)

    def row0(h, part):
        return h * (n * hr) + part * hr

    def gather_send(phase, h, buf, axis):
        me = x if axis == X else y
        for k in range(1, n):
            to = lax.rem(me + k, n)
            to = dev(at_x=to) if axis == X else dev(at_y=to)
            piece = cut(buf, row0(h, me), hr)
            copy = remote(piece, piece, ag_sem, (phase, h, k), to)
            copy.start()
            sent.append(copy)

    def gather_wait(phase, h, buf, axis):
        me = x if axis == X else y
        for k in range(1, n):
            piece = cut(buf, row0(h, lax.rem(me + n - k, n)), hr)
            remote(piece, piece, ag_sem, (phase, h, k), dev()).wait_recv()

    def swap_send(phase, h, src):
        dst = swap_buf.at[phase, h]

        @pl.when(x != y)
        def _():
            remote(src, dst, swap_sem, (phase, h), dev(at_x=y, at_y=x)).start()

        @pl.when(x == y)
        def _():
            dst[...] = src[...]

    def swap_wait(phase, h):
        dst = swap_buf.at[phase, h]

        @pl.when(x != y)
        def _():
            remote(dst, dst, swap_sem, (phase, h), dev(at_x=y, at_y=x)).wait_recv()

    def swap_sent(phase, h):
        dst = swap_buf.at[phase, h]

        @pl.when(x != y)
        def _():
            remote(dst, dst, swap_sem, (phase, h), dev(at_x=y, at_y=x)).wait_send()

    def stat_send(phase, h):
        stat_out[phase, h] = column[...].T[0:8, :]
        stat_in[phase, h, here] = stat_out[phase, h]

        def send(k):
            ax, ay = at(here + k)
            remote(
                stat_out.at[phase, h],
                stat_in.at[phase, h, here],
                stat_sem,
                (phase, h, k),
                dev(at_x=ax, at_y=ay),
            ).start()

        each(1, group, send)

    def stat_wait(phase, h, root_ref):
        def wait(k):
            source = lax.rem(here + group - k, group)
            piece = stat_in.at[phase, h, source]
            remote(piece, piece, stat_sem, (phase, h, k), dev()).wait_recv()

        each(1, group, wait)
        for part in range(n):
            total = stat_in[phase, h, part * n if phase == 1 else part]
            for c in range(1, n):
                index = part * n + c if phase == 1 else c * n + part
                total = total + stat_in[phase, h, index]
            root = lax.rsqrt(total / D + epsilon)
            root_ref[pl.ds(row0(h, part), hr), :] = jnp.broadcast_to(root[0:1, :], (128, hr)).T

    def act_rows(src, dst, root_ref, mod, start):
        for i in range(0, hr, STEP):
            at_rows = pl.ds(pl.multiple_of(start + i, 16), STEP)
            scale = 1.0 + wide(level[at_rows, :]) * mod[...]
            shaped = src[at_rows, :].astype(F32) * wide(root_ref[at_rows, :]) * scale
            dst[at_rows, :] = (shaped / (1.0 + jnp.exp(-shaped))).astype(BF16)

    def layer(phase, h, axis, term):
        me = x if axis == X else y

        def one(k):
            part = lax.rem(me + k, n)
            start = row0(h, part)
            piece = cut(part_out.at[phase], start, hr)
            piece[...] = term(start).astype(BF16)
            to = dev(at_x=part) if axis == X else dev(at_y=part)
            remote(piece, part_in.at[phase, h, k], rs_sem, (phase, h, k), to).start()

        each(1, n, one)
        own[phase, h] = term(row0(h, me))

    def layer_wait(phase, h):
        for k in range(1, n):
            piece = part_in.at[phase, h, k]
            remote(piece, piece, rs_sem, (phase, h, k), dev()).wait_recv()

    def layer_sum(phase, h, i):
        total = own[phase, h, pl.ds(i, STEP), :]
        for k in range(1, n):
            total = total + part_in[phase, h, k, pl.ds(i, STEP), :].astype(F32)
        return total

    def dot(a, b, over_a, over_b):
        return lax.dot_general(
            a, b, (((over_a,), (over_b,)), ((), ())), preferred_element_type=F32
        )

    def sums(i, value):
        total = jnp.sum(value, axis=1, keepdims=True)
        column[pl.ds(i, STEP), :] = jnp.broadcast_to(total, (STEP, 128))

    for h in range(H):
        for i in range(0, hr, STEP):
            local = pl.ds(h * hr + i, STEP)
            lev = wide(level[pl.ds(pl.multiple_of(row0(h, y) + i, 16), STEP), :])
            value = (1.0 - lev) * clean[local, :].astype(F32) + lev * cnoise[local, :].astype(F32)
            value = value.astype(BF16)
            noisy_all[pl.ds(pl.multiple_of(row0(h, y) + i, 16), STEP), :] = value
            value = value.astype(F32)
            sums(i, value * value)
        gather_send(0, h, noisy_all, Y)
        stat_send(0, h)
        swap_send(0, h, cut(noisy_all, row0(h, y), hr))

    w1[pl.ds(pl.multiple_of(z * wr, 16), wr), :] = w1_shard[...]

    def w1_copy(k):
        to = lax.rem(z + k, nz)
        return remote(w1_shard, cut(w1, z * wr, wr), w_sem, (0, k), dev(at_z=to))

    def w2_copy(k):
        to = lax.rem(z + k, nz)
        return remote(w2_shard, cut(w2, z * wr, wr), w_sem, (1, k), dev(at_x=y, at_z=to, at_y=x))

    each(1, nz, lambda k: w1_copy(k).start())
    each(1, nz, lambda k: w2_copy(k).start())

    @pl.when(x != y)
    def _():
        w2_copy(0).start()

    @pl.when(x == y)
    def _():
        w2[pl.ds(pl.multiple_of(z * wr, 16), wr), :] = w2_shard[...]

    def w_wait(which, full, low):
        def wait(k):
            piece = cut(full, lax.rem(z + nz - k, nz) * wr, wr)
            remote(piece, piece, w_sem, (which, k), dev()).wait_recv()

        each(low, nz, wait)

    for h in range(H):
        gather_wait(0, h, noisy_all, Y)
        stat_wait(0, h, root_q)
        each(0, n, lambda p, h=h: act_rows(noisy_all, first_all, root_q, mod_one, row0(h, p)))
        if h == 0:
            w_wait(0, w1, 1)
        layer(0, h, X, lambda s: dot(cut(first_all, s, hr)[...], w1[...], 1, 0))

    for h in range(H):
        layer_wait(0, h)
        swap_wait(0, h)
        for i in range(0, hr, STEP):
            value = swap_buf[0, h, pl.ds(i, STEP), :].astype(F32) + layer_sum(0, h, i)
            value = value.astype(BF16)
            hidden_all[pl.ds(pl.multiple_of(row0(h, x) + i, 16), STEP), :] = value
            value = value.astype(F32)
            sums(i, value * value)
        gather_send(1, h, hidden_all, X)
        stat_send(1, h)
        swap_send(1, h, cut(hidden_all, row0(h, x), hr))

    for h in range(H):
        gather_wait(1, h, hidden_all, X)
        stat_wait(1, h, root_p)
        each(0, n, lambda p, h=h: act_rows(hidden_all, second_all, root_p, mod_two, row0(h, p)))
        if h == 0:
            w_wait(1, w2, 1)

            @pl.when(x != y)
            def _():
                piece = cut(w2, z * wr, wr)
                remote(piece, piece, w_sem, (1, 0), dev()).wait_recv()

        layer(1, h, Y, lambda s: dot(cut(second_all, s, hr)[...], w2[...], 1, 0))

    def role_copy(h):
        return remote(pred.at[h], pred_other.at[h], role_sem, (h,), dev(role=1 - r))

    for h in range(H):
        layer_wait(1, h)
        swap_wait(1, h)
        for i in range(0, hr, STEP):
            local = pl.ds(h * hr + i, STEP)
            value = swap_buf[1, h, pl.ds(i, STEP), :].astype(F32) + layer_sum(1, h, i)
            value = value.astype(BF16)
            pred[h, pl.ds(i, STEP), :] = value
            target = cnoise[local, :].astype(F32) - clean[local, :].astype(F32)
            delta = ((value.astype(F32) - target) * wide(valid[local, :])).astype(BF16)
            delta_all[pl.ds(pl.multiple_of(row0(h, y) + i, 16), STEP), :] = delta
        gather_send(2, h, delta_all, Y)
        swap_send(2, h, cut(delta_all, row0(h, y), hr))
        role_copy(h).start()

    for h in range(H):
        gather_wait(2, h, delta_all, Y)
        layer(2, h, X, lambda s: dot(cut(delta_all, s, hr)[...], w2[...], 1, 1))

    half = width // 2

    def g_copy(which, out, into, block, k_to, swapped_place):
        to = dev(at_x=y, at_z=k_to, at_y=x) if swapped_place else dev(at_z=k_to)
        return pltpu.make_async_remote_copy(
            src_ref=cut(out, block * wr, wr),
            dst_ref=into.at[z],
            send_sem=g_sem.at[0, which, block],
            recv_sem=g_sem.at[1, which, z],
            device_id=to,
            device_id_type=MESH,
        )

    def g_send(which, out, into, part, swapped_place):
        def one(k):
            block = part * (nz // 2) + lax.rem(z + k, nz // 2)

            @pl.when((block != z) | ((x != y) & swapped_place))
            def _():
                g_copy(which, out, into, block, block, swapped_place).start()

        each(0, nz // 2, one)

    for part in range(2):
        columns = pl.ds(part * half, half)
        for j in range(0, width, half):
            g2_out[columns, pl.ds(j, half)] = dot(
                second_all[:, columns], delta_all[:, pl.ds(j, half)], 0, 0
            ).astype(BF16)
        g_send(1, g2_out, g2_in, part, True)

    def norm_parts(h, i):
        at_rows = pl.ds(pl.multiple_of(row0(h, x) + i, 16), STEP)
        scale = 1.0 + wide(level[at_rows, :]) * mod_two[...]
        root = wide(root_p[at_rows, :])
        normed = hidden_all[at_rows, :].astype(F32) * root
        shaped = normed * scale
        sig = sigmoid(shaped)
        grad = layer_sum(2, h, i) * (sig * (1.0 + shaped * (1.0 - sig))) * scale
        return root, normed, grad

    def inner_copy(h, k):
        to = lax.rem(y + k, n)
        return remote(inner_out.at[h], inner_in.at[h, y], inner_sem, (h, k), dev(at_y=to))

    for h in range(H):
        layer_wait(2, h)
        for i in range(0, hr, STEP):
            _, normed, grad = norm_parts(h, i)
            own[0, h, pl.ds(i, STEP), :] = grad
            sums(i, grad * normed)
        inner_out[h] = column[...].T[0:8, :]
        inner_in[h, y] = inner_out[h]
        for k in range(1, n):
            inner_copy(h, k).start()

    for h in range(H):
        for k in range(1, n):
            piece = inner_in.at[h, lax.rem(y + n - k, n)]
            remote(piece, piece, inner_sem, (h, k), dev()).wait_recv()
        total = inner_in[h, 0]
        for c in range(1, n):
            total = total + inner_in[h, c]
        column[...] = jnp.broadcast_to(total[0:1, :] / D, (128, hr)).T
        swap_wait(2, h)
        for i in range(0, hr, STEP):
            at_rows = pl.ds(pl.multiple_of(row0(h, x) + i, 16), STEP)
            root = wide(root_p[at_rows, :])
            normed = hidden_all[at_rows, :].astype(F32) * root
            grad = own[0, h, pl.ds(i, STEP), :]
            back = root * (grad - normed * wide(column[pl.ds(i, STEP), :]))
            value = swap_buf[2, h, pl.ds(i, STEP), :].astype(F32) + back
            up_all[at_rows, :] = value.astype(BF16)
        gather_send(3, h, up_all, X)

    for h in range(H):
        role_copy(h).wait_recv()
        for i in range(0, hr, STEP):
            lev = wide(level[pl.ds(pl.multiple_of(row0(h, y) + i, 16), STEP), :])
            mine = pred[h, pl.ds(i, STEP), :].astype(F32)
            other = pred_other[h, pl.ds(i, STEP), :].astype(F32)
            diff = jnp.where(r == 1, mine - other, other - mine)
            gap[pl.ds(h * hr + i, STEP), :] = ((1.0 - lev) * diff).astype(BF16)

    for h in range(H):
        gather_wait(3, h, up_all, X)
    for part in range(2):
        columns = pl.ds(part * half, half)
        for j in range(0, width, half):
            g1_out[columns, pl.ds(j, half)] = dot(
                first_all[:, columns], up_all[:, pl.ds(j, half)], 0, 0
            ).astype(BF16)
        g_send(0, g1_out, g1_in, part, False)
    g1_in[z] = g1_out[pl.ds(pl.multiple_of(z * wr, 16), wr), :]

    @pl.when(x == y)
    def _():
        g2_in[z] = g2_out[pl.ds(pl.multiple_of(z * wr, 16), wr), :]

    def g_finish(which, out, into, result, swapped_place):
        def wait(source):
            @pl.when((source != z) | ((x != y) & swapped_place))
            def _():
                piece = into.at[source]
                pltpu.make_async_remote_copy(
                    src_ref=piece,
                    dst_ref=piece,
                    send_sem=g_sem.at[0, which, source],
                    recv_sem=g_sem.at[1, which, source],
                    device_id=dev(),
                    device_id_type=MESH,
                ).wait_recv()

        each(0, nz, wait)
        for i in range(0, wr, STEP):
            total = into[0, pl.ds(i, STEP), :].astype(F32)
            for s in range(1, nz):
                total = total + into[s, pl.ds(i, STEP), :].astype(F32)
            result[pl.ds(i, STEP), :] = total

        def done(block):
            @pl.when((block != z) | ((x != y) & swapped_place))
            def _():
                g_copy(which, out, into, block, block, swapped_place).wait_send()

        each(0, nz, done)

    g_finish(1, g2_out, g2_in, grad_two, True)
    g_finish(0, g1_out, g1_in, grad_one, False)

    for copy in sent:
        copy.wait_send()
    each(1, nz, lambda k: w1_copy(k).wait_send())
    each(1, nz, lambda k: w2_copy(k).wait_send())

    @pl.when(x != y)
    def _():
        w2_copy(0).wait_send()

    for h in range(H):
        role_copy(h).wait_send()
        for phase in range(3):
            swap_sent(phase, h)

            def part_sent(k, phase=phase, h=h):
                piece = part_in.at[phase, h, k]
                remote(piece, piece, rs_sem, (phase, h, k), dev()).wait_send()

            each(1, n, part_sent)
        for phase in range(2):

            def stat_sent(k, phase=phase, h=h):
                piece = stat_out.at[phase, h]
                remote(piece, piece, stat_sem, (phase, h, k), dev()).wait_send()

            each(1, group, stat_sent)
        for k in range(1, n):
            inner_copy(h, k).wait_send()


def critic(n, nz, clean, cnoise, level, valid, mod_one, mod_two, w1_shard, w2_shard):
    rows, width = clean.shape
    hr = rows // H
    wr = w1_shard.shape[0]
    group = n * n
    vmem = pl.BlockSpec(memory_space=pltpu.VMEM)
    whole = pltpu.VMEM((n * rows, width), BF16)
    square = pltpu.VMEM((nz * wr, width), BF16)
    pieces = pltpu.VMEM((nz, wr, width), BF16)
    return pl.pallas_call(
        functools.partial(critic_kernel, n, nz),
        out_shape=(
            jax.ShapeDtypeStruct((rows, width), BF16),
            jax.ShapeDtypeStruct((wr, width), F32),
            jax.ShapeDtypeStruct((wr, width), F32),
        ),
        in_specs=[vmem] * 8,
        out_specs=(vmem,) * 3,
        scratch_shapes=[
            square,
            square,
            whole,
            whole,
            whole,
            whole,
            whole,
            whole,
            pltpu.VMEM((n * rows, 128), F32),
            pltpu.VMEM((n * rows, 128), F32),
            pltpu.VMEM((8, 128), BF16),
            pltpu.VMEM((H, hr, width), BF16),
            pltpu.VMEM((H, hr, width), BF16),
            pltpu.VMEM((3, H, hr, width), BF16),
            pltpu.VMEM((3, n * rows, width), BF16),
            pltpu.VMEM((3, H, n, hr, width), BF16),
            pltpu.VMEM((3, H, hr, width), F32),
            square,
            pieces,
            square,
            pieces,
            pltpu.VMEM((hr, 128), F32),
            pltpu.VMEM((2, H, 8, hr), F32),
            pltpu.VMEM((2, H, group, 8, hr), F32),
            pltpu.VMEM((H, 8, hr), F32),
            pltpu.VMEM((H, n, 8, hr), F32),
            pltpu.SemaphoreType.DMA((2, 2, nz)),
            pltpu.SemaphoreType.DMA((2, 4, H, n)),
            pltpu.SemaphoreType.DMA((2, 3, H, n)),
            pltpu.SemaphoreType.DMA((2, 3, H)),
            pltpu.SemaphoreType.DMA((2, 2, H, group)),
            pltpu.SemaphoreType.DMA((2, H, n)),
            pltpu.SemaphoreType.DMA((2, 2, nz)),
            pltpu.SemaphoreType.DMA((2, H)),
        ],
        compiler_params=pltpu.CompilerParams(
            collective_id=0, has_side_effects=True, vmem_limit_bytes=60 * 2**20
        ),
    )(clean, cnoise, level, valid, mod_one, mod_two, w1_shard, w2_shard)


def shards(
    noise,
    gen_gain,
    gen_weight,
    routes,
    critic_noise,
    critic_steps,
    crit_mod,
    crit_first,
    crit_second,
):
    width = noise.shape[1]
    groups = lax.axis_size(DP)
    x, y, z, role = (lax.axis_index(a) for a in (X, Y, Z, R))
    blocks_here = noise.shape[0] // BT
    most = 2 * blocks_here // groups

    gen_full = lax.all_gather(swapped(gen_weight), Z, axis=0, tiled=True)

    noise_q = swapped(noise)
    crit_noise_q = swapped(critic_noise)
    steps_all = collect_rows(critic_steps, X)
    level_all = jnp.repeat(steps_all.astype(F32) / levels, BT)[:, None]
    rows = critic_noise.shape[0]
    modulation = crit_mod[0]
    mod_one = columns_of(modulation[0], x, width)[None, :]
    mod_two = columns_of(modulation[1], y, width)[None, :]
    gain_y = columns_of(gen_gain, y, width)[None, :]

    gen_root = root_of(noise, Y)
    gen_root_all = collect_rows(gen_root[:, 0], X)[:, None]
    gen_act = act(collect_rows(noise, X), gen_root_all, gain_y)
    generated = (noise_q.astype(F32) + summed_rows_of(mm(gen_act, gen_full, 1, 0), Y)).astype(BF16)

    me_index = y * lax.axis_size(Z) + z
    table = routes[:, 0]
    target_index = lax.dynamic_slice_in_dim(table, me_index * blocks_here, blocks_here, 0)
    order = jnp.arange(blocks_here, dtype=jnp.int32)
    earlier = (target_index[:, None] == target_index[None, :]) & (order[None, :] < order[:, None])
    rank = jnp.sum(earlier.astype(jnp.int32), axis=1)
    slot_here = target_index * most + rank
    placing = (jnp.arange(groups * most, dtype=jnp.int32)[:, None] == slot_here[None, :]).astype(
        BF16
    )
    outgoing = jnp.dot(
        placing, generated.reshape(blocks_here, BT * width), preferred_element_type=F32
    )
    outgoing = outgoing.astype(BF16).reshape(groups, most * BT, width)
    incoming = lax.all_to_all(outgoing, YZ, split_axis=0, concat_axis=0, tiled=True)
    clean = incoming.reshape(groups * most * BT, width)
    counts = jnp.sum((table.reshape(groups, blocks_here) == me_index).astype(jnp.int32), axis=1)
    filled = (jnp.arange(most, dtype=jnp.int32)[None, :] < counts[:, None]).astype(F32)
    valid = jnp.repeat(filled.reshape(groups * most), BT)[:, None]

    level_wide = jnp.swapaxes(level_all.reshape(lax.axis_size(X), H, rows // H, 1), 0, 1)
    level_wide = jnp.broadcast_to(level_wide.reshape(-1, 1), (level_all.shape[0], 128))
    gap, grad_one, grad_two = critic(
        lax.axis_size(X),
        lax.axis_size(Z),
        clean,
        crit_noise_q,
        level_wide,
        jnp.broadcast_to(valid / TOK_DEV, (rows, 128)),
        mod_one,
        mod_two,
        crit_first[0],
        crit_second[0],
    )
    gap = gap.reshape(groups, most * BT, width)
    coming_back = lax.all_to_all(gap, YZ, split_axis=0, concat_axis=0, tiled=True)
    picked = mm(placing, coming_back.reshape(groups * most, BT * width), 0, 0)
    returned = picked.astype(BF16).reshape(blocks_here * BT, width)

    half = width // 2
    mine = lambda array: columns_of(array, role, half)
    weight_half = lax.dynamic_slice_in_dim(gen_full, role * half, half, 0)
    gen_owned = summed_rows_of(mm(collect_rows(returned, Y), weight_half, 1, 1), X)
    normed, shaped = shaped_of(mine(noise), gen_root, mine(gain_y))
    grad_norm = gen_owned * slope(shaped) * mine(gain_y)
    inner = of_everyone(jnp.sum(grad_norm * normed, axis=-1)[None], (R, Y))[0][:, None]
    back = gen_root * (grad_norm - normed * (inner / D))
    noise_grad = mine(swapped(returned)).astype(F32) + back
    return (noise_grad.reshape(-1, 1, 1, half), grad_one[None], grad_two[None])


def solution(mesh):
    split = Mesh(
        mesh.devices.reshape(mesh.shape[R], mesh.shape[Y], -1, mesh.shape[Y]),
        (R, X, Z, Y),
    )
    in_specs = (
        P(DP, Y),
        P(),
        P(DP, Y),
        P(),
        P(DP, Y),
        P(DP),
        P(R, None, None),
        P(R, DP, Y),
        P(R, DP, Y),
    )
    out_specs = (P(DP, Y, R, None), P(R, DP, Y), P(R, DP, Y))
    return jax.shard_map(
        shards, mesh=split, in_specs=in_specs, out_specs=out_specs, check_vma=False
    )
```

```python
import functools

import jax
import jax.numpy as jnp
from jax import lax
from jax.experimental import pallas as pl
from jax.experimental.pallas import tpu as pltpu
from jax.sharding import Mesh
from jax.sharding import PartitionSpec as P

D = 3072
TOK_DEV = 128
BT = 4
R, X, Z, Y = "role", "dp_0", "dp_1", "mp"
DP = (X, Z)
YZ = (Y, Z)
F32, BF16 = jnp.float32, jnp.bfloat16

epsilon = 1e-06
levels = 1000.0


def columns_of(array, index, width):
    return lax.dynamic_slice_in_dim(array, index * width, width, array.ndim - 1)


H = 2
STEP = 32
MESH = pl.DeviceIdType.MESH


def sigmoid(v):
    return 1.0 / (1.0 + jnp.exp(-v))


def step_kernel(
    n,
    nz,
    noise,
    gain,
    wg_shard,
    place,
    place_back,
    cnoise_p,
    level_rows,
    valid,
    mod_one,
    mod_two,
    w1_shard,
    w2_shard,
    noise_grad,
    grad_one,
    grad_two,
    w1,
    w2,
    noisy_all,
    first_all,
    hidden_all,
    second_all,
    delta_all,
    up_all,
    root_q,
    root_p,
    level,
    clean,
    cnoise,
    pred,
    pred_other,
    swap_buf,
    part_out,
    part_in,
    own,
    g1_out,
    g1_in,
    g2_out,
    g2_in,
    column,
    stat_out,
    stat_in,
    inner_out,
    inner_in,
    level_in,
    wg,
    w2_mine,
    noise_in,
    noise_swap,
    gen_act,
    root_g,
    gen_made,
    gen_out,
    gen_in,
    gen_own,
    clean_out,
    clean_in,
    clean_other,
    gap,
    back_in,
    returned,
    ret_all,
    ret_swap,
    back_out,
    back_parts,
    back_own,
    gen_inner_out,
    gen_inner_in,
    g2_mine,
    g2_swap,
    w_sem,
    ag_sem,
    rs_sem,
    swap_sem,
    stat_sem,
    inner_sem,
    g_sem,
    role_sem,
    level_sem,
    wg_sem,
    wg_role_sem,
    one_sem,
    gen_sem,
    all_sem,
    noisy_sem,
    gen_inner_sem,
):
    r, x, z, y = (lax.axis_index(a) for a in (R, X, Z, Y))
    rows, width = cnoise.shape
    hr = rows // H
    wr = w1_shard.shape[0]
    toks = noise.shape[0]
    th = toks // 2
    half = width // 2
    groups = n * nz
    lanes = width // 128
    group = n * n
    here = x * n + y

    def dev(role=r, at_x=x, at_z=z, at_y=y):
        return (role, at_x, at_z, at_y)

    def remote(src, dst, sems, index, to):
        return pltpu.make_async_remote_copy(
            src_ref=src,
            dst_ref=dst,
            send_sem=sems.at[(0, *index)],
            recv_sem=sems.at[(1, *index)],
            device_id=to,
            device_id_type=MESH,
        )

    sent = []

    def each(low, high, body):
        def step(k, carry):
            body(k)
            return carry

        lax.fori_loop(low, high, step, 0)

    def wide(narrow):
        return jnp.concatenate([narrow] * lanes, axis=1)

    def cut(ref, start, count):
        return ref.at[pl.ds(pl.multiple_of(start, 16), count), :]

    barrier = pltpu.get_barrier_semaphore()

    def greet(to):
        pl.semaphore_signal(barrier, inc=1, device_id=to, device_id_type=MESH)

    def at(index):
        index = lax.rem(index, group)
        return index // n, lax.rem(index, n)

    def greet_plane(k):
        ax, ay = at(here + k)
        greet(dev(at_x=ax, at_y=ay))

    def greet_z(k):
        az = lax.rem(z + k, nz)
        greet(dev(at_x=y, at_z=az, at_y=x))

    my_yz = y * nz + z

    def yz(index):
        index = lax.rem(index, groups)
        return index // nz, lax.rem(index, nz)

    def greet_yz(k):
        ay, az = yz(my_yz + k)
        greet(dev(at_y=ay, at_z=az))

    each(1, group, greet_plane)
    each(1, nz, greet_z)
    each(1, groups, greet_yz)
    each(0, n, lambda k: greet(dev(role=1 - r, at_y=lax.rem(y + k, n))))
    pl.semaphore_wait(barrier, group - 1 + nz - 1 + groups - 1 + n)

    wh = wr // 2
    other = dev(role=1 - r)

    def wg_piece(source, role):
        return cut(wg, source * wr + role * wh, wh)

    def wg_copy(k):
        to = dev(at_x=y, at_z=lax.rem(z + k, nz), at_y=x)
        return remote(cut(wg_shard, r * wh, wh), wg_piece(z, r), wg_sem, (k,), to)

    each(1, nz, lambda k: wg_copy(k).start())

    def swapping(copy, src, dst):
        @pl.when(x != y)
        def _():
            copy.start()

        @pl.when(x == y)
        def _():
            dst[...] = src[...]

    swapping(wg_copy(0), cut(wg_shard, r * wh, wh), wg_piece(z, r))
    noise_mine = cut(noise, r * th, th)

    def noise_copy(k):
        to = dev(at_x=lax.rem(x + k, n))
        return remote(noise_mine, noise_in.at[x], gen_sem, (0, k), to)

    for k in range(1, n):
        noise_copy(k).start()
    across = dev(at_x=y, at_y=x)
    noise_swap_copy = remote(noise_mine, noise_swap, one_sem, (0,), across)
    swapping(noise_swap_copy, noise_mine, noise_swap)

    def row0(h, part):
        return h * (n * hr) + part * hr

    def gather_send(phase, h, buf, axis):
        me = x if axis == X else y
        for k in range(1, n):
            to = lax.rem(me + k, n)
            to = dev(at_x=to) if axis == X else dev(at_y=to)
            piece = cut(buf, row0(h, me), hr)
            copy = remote(piece, piece, ag_sem, (phase, h, k), to)
            copy.start()
            sent.append(copy)

    def gather_wait(phase, h, buf, axis):
        me = x if axis == X else y
        for k in range(1, n):
            piece = cut(buf, row0(h, lax.rem(me + n - k, n)), hr)
            remote(piece, piece, ag_sem, (phase, h, k), dev()).wait_recv()

    def swap_send(phase, h, src):
        dst = swap_buf.at[phase, h]

        @pl.when(x != y)
        def _():
            remote(src, dst, swap_sem, (phase, h), dev(at_x=y, at_y=x)).start()

        @pl.when(x == y)
        def _():
            dst[...] = src[...]

    def swap_wait(phase, h):
        dst = swap_buf.at[phase, h]

        @pl.when(x != y)
        def _():
            remote(dst, dst, swap_sem, (phase, h), dev(at_x=y, at_y=x)).wait_recv()

    def swap_sent(phase, h):
        dst = swap_buf.at[phase, h]

        @pl.when(x != y)
        def _():
            remote(dst, dst, swap_sem, (phase, h), dev(at_x=y, at_y=x)).wait_send()

    def stat_send(phase, h):
        summed = column[...].T[0:8, :]
        stat_out[phase, h] = summed
        stat_in[phase, h, here] = summed

        def send(k):
            ax, ay = at(here + k)
            remote(
                stat_out.at[phase, h],
                stat_in.at[phase, h, here],
                stat_sem,
                (phase, h, k),
                dev(at_x=ax, at_y=ay),
            ).start()

        each(1, group, send)

    def stat_wait(phase, h, root_ref):
        def wait(k):
            source = lax.rem(here + group - k, group)
            piece = stat_in.at[phase, h, source]
            remote(piece, piece, stat_sem, (phase, h, k), dev()).wait_recv()

        each(1, group, wait)
        for part in range(n):
            start = part * hr if phase == 2 else row0(h, part)
            total = stat_in[phase, h, part * n if phase else part]
            for c in range(1, n):
                index = part * n + c if phase else c * n + part
                total = total + stat_in[phase, h, index]
            root = lax.rsqrt(total / D + epsilon)
            root_ref[pl.ds(start, hr), :] = jnp.broadcast_to(root[0:1, :], (128, hr)).T

    def act_rows(src, dst, root_ref, mod, start):
        for i in range(0, hr, STEP):
            at_rows = pl.ds(pl.multiple_of(start + i, 16), STEP)
            scale = 1.0 + wide(level[at_rows, :]) * mod[...]
            shaped = src[at_rows, :].astype(F32) * wide(root_ref[at_rows, :]) * scale
            dst[at_rows, :] = (shaped / (1.0 + jnp.exp(-shaped))).astype(BF16)

    def layer(phase, h, axis, term):
        me = x if axis == X else y

        def one(k):
            part = lax.rem(me + k, n)
            start = row0(h, part)
            piece = cut(part_out.at[phase], start, hr)
            piece[...] = term(start).astype(BF16)
            to = dev(at_x=part) if axis == X else dev(at_y=part)
            remote(piece, part_in.at[phase, h, k], rs_sem, (phase, h, k), to).start()

        each(1, n, one)
        own[phase, h] = term(row0(h, me))

    def layer_wait(phase, h):
        for k in range(1, n):
            piece = part_in.at[phase, h, k]
            remote(piece, piece, rs_sem, (phase, h, k), dev()).wait_recv()

    def layer_sum(phase, h, i):
        total = own[phase, h, pl.ds(i, STEP), :]
        for k in range(1, n):
            total = total + part_in[phase, h, k, pl.ds(i, STEP), :].astype(F32)
        return total

    def dot(a, b, over_a, over_b):
        return lax.dot_general(
            a, b, (((over_a,), (over_b,)), ((), ())), preferred_element_type=F32
        )

    def sums(i, value):
        total = jnp.sum(value, axis=1, keepdims=True)
        column[pl.ds(i, STEP), :] = jnp.broadcast_to(total, (STEP, 128))

    for i in range(0, toks, STEP):
        value = noise[pl.ds(i, STEP), :].astype(F32)
        sums(i, value * value)
    stat_send(2, 0)

    w1[pl.ds(pl.multiple_of(z * wr, 16), wr), :] = w1_shard[...]

    def w1_copy(k):
        to = lax.rem(z + k, nz)
        return remote(w1_shard, cut(w1, z * wr, wr), w_sem, (0, k), dev(at_z=to))

    def w2_copy(k):
        to = lax.rem(z + k, nz)
        return remote(w2_mine, cut(w2, z * wr, wr), w_sem, (1, k), dev(at_z=to))

    def w_wait(which, full):
        def wait(k):
            piece = cut(full, lax.rem(z + nz - k, nz) * wr, wr)
            remote(piece, piece, w_sem, (which, k), dev()).wait_recv()

        each(1, nz, wait)

    def level_copy(k):
        to = dev(at_x=lax.rem(x + k, n))
        return remote(level_rows, level_in.at[x], level_sem, (k,), to)

    for k in range(1, n):
        level_copy(k).start()
    level_in[x] = level_rows[...]
    w2_swap = remote(w2_shard, w2_mine, one_sem, (1,), across)
    swapping(w2_swap, w2_shard, w2_mine)
    cnoise_swap = remote(cnoise_p, cnoise, one_sem, (2,), across)
    swapping(cnoise_swap, cnoise_p, cnoise)
    each(1, nz, lambda k: w1_copy(k).start())

    def arrived(copy):
        @pl.when(x != y)
        def _():
            copy.wait_recv()

    noise_in[x] = noise_mine[...]
    for k in range(1, n):
        piece = noise_in.at[lax.rem(x + n - k, n)]
        remote(piece, piece, gen_sem, (0, k), dev()).wait_recv()
    stat_wait(2, 0, root_g)

    def gen_rows(part):
        for i in range(0, th, STEP):
            at_rows = pl.ds(pl.multiple_of(part * toks + r * th + i, 16), STEP)
            shaped = noise_in[part, pl.ds(i, STEP), :].astype(F32) * wide(root_g[at_rows, :])
            shaped = shaped * gain[...]
            gen_act[part, pl.ds(i, STEP), :] = (shaped / (1.0 + jnp.exp(-shaped))).astype(BF16)

    each(0, n, gen_rows)

    def wg_role(source):
        return remote(
            wg_piece(source, r), wg_piece(source, r), wg_role_sem, (source,), other
        )

    def wg_on(k):
        source = lax.rem(z + nz - k, nz)
        piece = wg_piece(source, r)
        remote(piece, piece, wg_sem, (k,), dev()).wait_recv()
        wg_role(source).start()

    each(1, nz, wg_on)

    @pl.when(x != y)
    def _():
        piece = wg_piece(z, r)
        remote(piece, piece, wg_sem, (0,), dev()).wait_recv()

    wg_role(z).start()

    def wg_other(source):
        piece = wg_piece(source, 1 - r)
        remote(piece, piece, wg_role_sem, (source,), other).wait_recv()

    each(0, nz, wg_other)

    def gen_copy(k):
        part = lax.rem(y + k, n)
        return remote(gen_out.at[k], gen_in.at[k], gen_sem, (1, k), dev(at_y=part))

    def gen_part(k):
        part = lax.rem(y + k, n)
        gen_out[k] = dot(gen_act[part], wg[...], 1, 0).astype(BF16)
        gen_copy(k).start()

    each(1, n, gen_part)
    gen_own[...] = dot(gen_act[y], wg[...], 1, 0)
    for k in range(1, n):
        gen_copy(k).wait_recv()
    arrived(noise_swap_copy)
    for i in range(0, th, STEP):
        at_rows = pl.ds(i, STEP)
        total = noise_swap[at_rows, :].astype(F32) + gen_own[at_rows, :]
        for k in range(1, n):
            total = total + gen_in[k, at_rows, :].astype(F32)
        gen_made[at_rows, :] = total.astype(BF16)

    gr = rows // groups
    per = hr // gr
    for h in range(H):
        placed = dot(place[pl.ds(h * hr, hr), :], gen_made[...], 1, 0).astype(BF16)
        clean_out[pl.ds(h * per, per)] = placed.reshape(per, gr, width)

    def clean_copy(k):
        index = lax.rem(my_yz + k, groups)
        ay, az = yz(index)
        return remote(
            clean_out.at[index], clean_in.at[my_yz], all_sem, (0, k), dev(at_y=ay, at_z=az)
        )

    each(1, groups, lambda k: clean_copy(k).start())
    clean_in[my_yz] = clean_out[my_yz]

    arrived(w2_swap)
    w2[pl.ds(pl.multiple_of(z * wr, 16), wr), :] = w2_mine[...]
    each(1, nz, lambda k: w2_copy(k).start())
    for k in range(1, n):
        piece = level_in.at[lax.rem(x + n - k, n)]
        remote(piece, piece, level_sem, (k,), dev()).wait_recv()
    for h in range(H):
        for part in range(n):
            line = level_in[part, h]
            level[pl.ds(row0(h, part), hr), :] = jnp.broadcast_to(line[0:1, :], (128, hr)).T
    arrived(cnoise_swap)

    def clean_wait(k):
        piece = clean_in.at[lax.rem(my_yz + groups - k, groups)]
        remote(piece, piece, all_sem, (0, k), dev()).wait_recv()

    each(1, groups, clean_wait)
    clean_role = remote(clean_in, clean_other, one_sem, (3,), other)
    clean_role.start()
    clean_role.wait_recv()

    rh = hr // 2

    def noisy_piece(h, part, role):
        return cut(noisy_all, row0(h, part) + role * rh, rh)

    def noisy_copy(h, k):
        piece = noisy_piece(h, y, r)
        return remote(piece, piece, ag_sem, (0, h, k), dev(at_y=lax.rem(y + k, n)))

    def noisy_role(h, k):
        piece = noisy_piece(h, lax.rem(y + n - k, n), r)
        return remote(piece, piece, noisy_sem, (h, k), other)

    for h in range(H):
        for i in range(0, hr, STEP):
            local = pl.ds(h * hr + i, STEP)
            if gr <= STEP:
                some = pl.ds((h * hr + i) // gr, STEP // gr)
                value = clean_in[some].astype(F32) + clean_other[some].astype(F32)
            else:
                some = (h * hr + i) // gr, pl.ds((h * hr + i) % gr, STEP)
                value = clean_in[some].astype(F32) + clean_other[some].astype(F32)
            value = value.reshape(STEP, width)
            clean[local, :] = value.astype(BF16)
            lev = wide(level[pl.ds(pl.multiple_of(row0(h, y) + i, 16), STEP), :])
            value = (1.0 - lev) * value + lev * cnoise[local, :].astype(F32)
            value = value.astype(BF16)
            noisy_all[pl.ds(pl.multiple_of(row0(h, y) + i, 16), STEP), :] = value
            value = value.astype(F32)
            sums(i, value * value)
        for k in range(1, n):
            noisy_copy(h, k).start()
        stat_send(0, h)
        swap_send(0, h, cut(noisy_all, row0(h, y), hr))

    def noisy_wait(h):
        for k in range(1, n):
            piece = noisy_piece(h, lax.rem(y + n - k, n), r)
            remote(piece, piece, ag_sem, (0, h, k), dev()).wait_recv()
            noisy_role(h, k).start()
        for k in range(1, n):
            piece = noisy_piece(h, lax.rem(y + n - k, n), 1 - r)
            remote(piece, piece, noisy_sem, (h, k), other).wait_recv()

    for h in range(H):
        noisy_wait(h)
        stat_wait(0, h, root_q)
        each(0, n, lambda p, h=h: act_rows(noisy_all, first_all, root_q, mod_one, row0(h, p)))
        if h == 0:
            w_wait(0, w1)
        layer(0, h, X, lambda s: dot(cut(first_all, s, hr)[...], w1[...], 1, 0))

    for h in range(H):
        layer_wait(0, h)
        swap_wait(0, h)
        for i in range(0, hr, STEP):
            value = swap_buf[0, h, pl.ds(i, STEP), :].astype(F32) + layer_sum(0, h, i)
            value = value.astype(BF16)
            hidden_all[pl.ds(pl.multiple_of(row0(h, x) + i, 16), STEP), :] = value
            value = value.astype(F32)
            sums(i, value * value)
        gather_send(1, h, hidden_all, X)
        stat_send(1, h)
        swap_send(1, h, cut(hidden_all, row0(h, x), hr))

    for h in range(H):
        gather_wait(1, h, hidden_all, X)
        stat_wait(1, h, root_p)
        each(0, n, lambda p, h=h: act_rows(hidden_all, second_all, root_p, mod_two, row0(h, p)))
        if h == 0:
            w_wait(1, w2)
        layer(1, h, Y, lambda s: dot(cut(second_all, s, hr)[...], w2[...], 1, 0))

    def role_copy(h):
        return remote(pred.at[h], pred_other.at[h], role_sem, (h,), dev(role=1 - r))

    for h in range(H):
        layer_wait(1, h)
        swap_wait(1, h)
        for i in range(0, hr, STEP):
            local = pl.ds(h * hr + i, STEP)
            value = swap_buf[1, h, pl.ds(i, STEP), :].astype(F32) + layer_sum(1, h, i)
            value = value.astype(BF16)
            pred[h, pl.ds(i, STEP), :] = value
            target = cnoise[local, :].astype(F32) - clean[local, :].astype(F32)
            delta = ((value.astype(F32) - target) * wide(valid[local, :])).astype(BF16)
            delta_all[pl.ds(pl.multiple_of(row0(h, y) + i, 16), STEP), :] = delta
        gather_send(2, h, delta_all, Y)
        swap_send(2, h, cut(delta_all, row0(h, y), hr))
        role_copy(h).start()

    for h in range(H):
        gather_wait(2, h, delta_all, Y)
        layer(2, h, X, lambda s: dot(cut(delta_all, s, hr)[...], w2[...], 1, 1))

    def g_copy(which, out, into, block):
        return pltpu.make_async_remote_copy(
            src_ref=cut(out, block * wr, wr),
            dst_ref=into.at[z],
            send_sem=g_sem.at[0, which, block],
            recv_sem=g_sem.at[1, which, z],
            device_id=dev(at_z=block),
            device_id_type=MESH,
        )

    def g_term(which, left, right, out, into):
        for part in range(2):
            columns = pl.ds(part * half, half)
            for j in range(0, width, half):
                out[columns, pl.ds(j, half)] = dot(
                    left[:, columns], right[:, pl.ds(j, half)], 0, 0
                ).astype(BF16)

            def one(k, part=part):
                block = part * (nz // 2) + lax.rem(z + k, nz // 2)

                @pl.when(block != z)
                def _():
                    g_copy(which, out, into, block).start()

            each(0, nz // 2, one)
        into[z] = out[pl.ds(pl.multiple_of(z * wr, 16), wr), :]

    g_term(1, second_all, delta_all, g2_out, g2_in)

    for h in range(H):
        role_copy(h).wait_recv()
        for i in range(0, hr, max(STEP, gr)):
            count = max(STEP, gr)
            lev = wide(level[pl.ds(pl.multiple_of(row0(h, y) + i, 16), count), :])
            mine = pred[h, pl.ds(i, count), :].astype(F32)
            theirs = pred_other[h, pl.ds(i, count), :].astype(F32)
            diff = jnp.where(r == 1, mine - theirs, theirs - mine)
            diff = ((1.0 - lev) * diff).astype(BF16)
            some = pl.ds((h * hr + i) // gr, count // gr)
            for c in range(2):
                gap[c, some] = diff[:, c * half : (c + 1) * half].reshape(count // gr, gr, half)

    def back_copy(k):
        index = lax.rem(my_yz + k, groups)
        ay, az = yz(index)
        return remote(
            gap.at[r, index], back_in.at[my_yz], all_sem, (1, k), dev(at_y=ay, at_z=az)
        )

    each(1, groups, lambda k: back_copy(k).start())
    back_in[my_yz] = gap[r, my_yz]

    def norm_parts(h, i):
        at_rows = pl.ds(pl.multiple_of(row0(h, x) + i, 16), STEP)
        scale = 1.0 + wide(level[at_rows, :]) * mod_two[...]
        root = wide(root_p[at_rows, :])
        normed = hidden_all[at_rows, :].astype(F32) * root
        shaped = normed * scale
        sig = sigmoid(shaped)
        grad = layer_sum(2, h, i) * (sig * (1.0 + shaped * (1.0 - sig))) * scale
        return root, normed, grad

    def inner_copy(h, k):
        to = lax.rem(y + k, n)
        return remote(inner_out.at[h], inner_in.at[h, y], inner_sem, (h, k), dev(at_y=to))

    for h in range(H):
        layer_wait(2, h)
        for i in range(0, hr, STEP):
            _, normed, grad = norm_parts(h, i)
            own[0, h, pl.ds(i, STEP), :] = grad
            sums(i, grad * normed)
        inner_out[h] = column[...].T[0:8, :]
        inner_in[h, y] = inner_out[h]
        for k in range(1, n):
            inner_copy(h, k).start()

    for h in range(H):
        for k in range(1, n):
            piece = inner_in.at[h, lax.rem(y + n - k, n)]
            remote(piece, piece, inner_sem, (h, k), dev()).wait_recv()
        total = inner_in[h, 0]
        for c in range(1, n):
            total = total + inner_in[h, c]
        column[...] = jnp.broadcast_to(total[0:1, :] / D, (128, hr)).T
        swap_wait(2, h)
        for i in range(0, hr, STEP):
            at_rows = pl.ds(pl.multiple_of(row0(h, x) + i, 16), STEP)
            root = wide(root_p[at_rows, :])
            normed = hidden_all[at_rows, :].astype(F32) * root
            grad = own[0, h, pl.ds(i, STEP), :]
            back = root * (grad - normed * wide(column[pl.ds(i, STEP), :]))
            value = swap_buf[2, h, pl.ds(i, STEP), :].astype(F32) + back
            up_all[at_rows, :] = value.astype(BF16)
        gather_send(3, h, up_all, X)

    def back_wait(k):
        piece = back_in.at[lax.rem(my_yz + groups - k, groups)]
        remote(piece, piece, all_sem, (1, k), dev()).wait_recv()

    each(1, groups, back_wait)
    slots = back_in[...].reshape(rows, half)
    returned[r] = dot(place_back[...], slots, 1, 0).astype(BF16)
    ret_role = remote(returned.at[r], returned.at[r], one_sem, (4,), other)
    ret_role.start()
    ret_swap_copy = remote(returned.at[r], ret_swap, one_sem, (5,), across)
    swapping(ret_swap_copy, returned.at[r], ret_swap)
    theirs = returned.at[1 - r]
    remote(theirs, theirs, one_sem, (4,), other).wait_recv()
    ret_all[y] = returned[...]

    def ret_copy(k):
        return remote(returned, ret_all.at[y], gen_sem, (2, k), dev(at_y=lax.rem(y + k, n)))

    for k in range(1, n):
        ret_copy(k).start()

    for h in range(H):
        gather_wait(3, h, up_all, X)
    g_term(0, first_all, up_all, g1_out, g1_in)

    for k in range(1, n):
        piece = ret_all.at[lax.rem(y + n - k, n)]
        remote(piece, piece, gen_sem, (2, k), dev()).wait_recv()

    def back_part_copy(k):
        to = dev(at_x=lax.rem(x + k, n))
        return remote(back_out.at[k], back_parts.at[k], gen_sem, (3, k), to)

    def back_part(k):
        part = lax.rem(x + k, n)
        total = dot(ret_all[part, 0], weight_half(0), 1, 1)
        total = total + dot(ret_all[part, 1], weight_half(1), 1, 1)
        return total

    def weight_half(c):
        return wg[pl.ds(pl.multiple_of(r * half, 16), half), pl.ds(c * half, half)]

    def back_send(k):
        back_out[k] = back_part(k).astype(BF16)
        back_part_copy(k).start()

    each(1, n, back_send)
    back_own[...] = back_part(0)
    for k in range(1, n):
        back_part_copy(k).wait_recv()

    def my_half(ref, at_rows):
        low, high = ref[at_rows, pl.ds(0, half)], ref[at_rows, pl.ds(half, half)]
        return jnp.where(r == 1, high.astype(F32), low.astype(F32))

    def narrow(value):
        return jnp.concatenate([value] * (half // 128), axis=1)

    def gen_normed(i):
        at_rows = pl.ds(i, STEP)
        root = narrow(root_g[pl.ds(pl.multiple_of(x * toks + i, 16), STEP), :])
        return root, my_half(noise, at_rows) * root

    gain_half = my_half(gain, pl.ds(0, 1))
    for i in range(0, toks, STEP):
        at_rows = pl.ds(i, STEP)
        _, normed = gen_normed(i)
        shaped = normed * gain_half
        sig = sigmoid(shaped)
        total = back_own[at_rows, :]
        for k in range(1, n):
            total = total + back_parts[k, at_rows, :].astype(F32)
        grad = total * (sig * (1.0 + shaped * (1.0 - sig))) * gain_half
        back_own[at_rows, :] = grad
        sums(i, grad * normed)
    summed = column[...].T[0:8, :]
    gen_inner_out[...] = summed
    spot = r * n + y
    gen_inner_in[spot] = summed

    def gen_inner_copy(k):
        index = lax.rem(spot + k, 2 * n)
        to = dev(role=index // n, at_y=lax.rem(index, n))
        return remote(gen_inner_out, gen_inner_in.at[spot], gen_inner_sem, (k,), to)

    for k in range(1, 2 * n):
        gen_inner_copy(k).start()
    for k in range(1, 2 * n):
        piece = gen_inner_in.at[lax.rem(spot + 2 * n - k, 2 * n)]
        remote(piece, piece, gen_inner_sem, (k,), dev()).wait_recv()
    total = gen_inner_in[0]
    for c in range(1, 2 * n):
        total = total + gen_inner_in[c]
    column[...] = jnp.broadcast_to(total[0:1, :] / D, (128, toks)).T
    arrived(ret_swap_copy)
    for i in range(0, toks, STEP):
        at_rows = pl.ds(i, STEP)
        root, normed = gen_normed(i)
        back = root * (back_own[at_rows, :] - normed * narrow(column[at_rows, :]))
        noise_grad[at_rows, :] = ret_swap[at_rows, :].astype(F32) + back

    def g_finish(which, into, result):
        def wait(source):
            @pl.when(source != z)
            def _():
                piece = into.at[source]
                pltpu.make_async_remote_copy(
                    src_ref=piece,
                    dst_ref=piece,
                    send_sem=g_sem.at[0, which, source],
                    recv_sem=g_sem.at[1, which, source],
                    device_id=dev(),
                    device_id_type=MESH,
                ).wait_recv()

        each(0, nz, wait)
        for i in range(0, wr, STEP):
            total = into[0, pl.ds(i, STEP), :].astype(F32)
            for s in range(1, nz):
                total = total + into[s, pl.ds(i, STEP), :].astype(F32)
            result[pl.ds(i, STEP), :] = total.astype(result.dtype)

    g_finish(1, g2_in, g2_mine)
    g2_swap_copy = remote(g2_mine, g2_swap, one_sem, (6,), across)
    swapping(g2_swap_copy, g2_mine, g2_swap)
    g_finish(0, g1_in, grad_one)
    arrived(g2_swap_copy)
    grad_two[...] = g2_swap[...].astype(F32)

    def g_sent(which, out, into):
        def done(block):
            @pl.when(block != z)
            def _():
                g_copy(which, out, into, block).wait_send()

        each(0, nz, done)

    g_sent(1, g2_out, g2_in)
    g_sent(0, g1_out, g1_in)

    for copy in sent:
        copy.wait_send()
    each(1, nz, lambda k: w1_copy(k).wait_send())
    each(1, nz, lambda k: w2_copy(k).wait_send())

    each(1, nz, lambda k: wg_copy(k).wait_send())
    each(0, nz, lambda k: wg_role(k).wait_send())
    each(1, groups, lambda k: clean_copy(k).wait_send())
    each(1, groups, lambda k: back_copy(k).wait_send())
    clean_role.wait_send()
    ret_role.wait_send()
    each(1, group, lambda k: remote(
        stat_out.at[2, 0], stat_out.at[2, 0], stat_sem, (2, 0, k), dev()
    ).wait_send())

    @pl.when(x != y)
    def _():
        wg_copy(0).wait_send()
        for copy in (noise_swap_copy, w2_swap, cnoise_swap, ret_swap_copy, g2_swap_copy):
            copy.wait_send()

    for k in range(1, n):
        for copy in (noise_copy, level_copy, gen_copy, ret_copy, back_part_copy):
            copy(k).wait_send()
    for k in range(1, 2 * n):
        gen_inner_copy(k).wait_send()

    for h in range(H):
        role_copy(h).wait_send()
        for k in range(1, n):
            noisy_copy(h, k).wait_send()
            noisy_role(h, k).wait_send()
        for phase in range(3):
            swap_sent(phase, h)

            def part_sent(k, phase=phase, h=h):
                piece = part_in.at[phase, h, k]
                remote(piece, piece, rs_sem, (phase, h, k), dev()).wait_send()

            each(1, n, part_sent)
        for phase in range(2):

            def stat_sent(k, phase=phase, h=h):
                piece = stat_out.at[phase, h]
                remote(piece, piece, stat_sem, (phase, h, k), dev()).wait_send()

            each(1, group, stat_sent)
        for k in range(1, n):
            inner_copy(h, k).wait_send()


def step(n, nz, *operands):
    noise, cnoise, w1_shard = operands[0], operands[5], operands[10]
    toks, width = noise.shape
    rows = cnoise.shape[0]
    hr, th, half = rows // H, toks // 2, width // 2
    wr = w1_shard.shape[0]
    group, groups = n * n, n * nz
    gr = rows // groups
    vmem = pl.BlockSpec(memory_space=pltpu.VMEM)
    bf = lambda *shape: pltpu.VMEM(shape, BF16)
    fl = lambda *shape: pltpu.VMEM(shape, F32)
    sems = lambda *shape: pltpu.SemaphoreType.DMA((2, *shape))
    whole = bf(n * rows, width)
    square = bf(nz * wr, width)
    pieces = bf(nz, wr, width)
    return pl.pallas_call(
        functools.partial(step_kernel, n, nz),
        out_shape=(
            jax.ShapeDtypeStruct((toks, half), F32),
            jax.ShapeDtypeStruct((wr, width), F32),
            jax.ShapeDtypeStruct((wr, width), F32),
        ),
        in_specs=[vmem] * 12,
        out_specs=(vmem,) * 3,
        scratch_shapes=[
            square,
            square,
            *[whole] * 6,
            fl(n * rows, 128),
            fl(n * rows, 128),
            fl(n * rows, 128),
            bf(rows, width),
            bf(rows, width),
            bf(H, hr, width),
            bf(H, hr, width),
            bf(3, H, hr, width),
            bf(3, n * rows, width),
            bf(3, H, n, hr, width),
            fl(3, H, hr, width),
            square,
            pieces,
            square,
            pieces,
            fl(hr, 128),
            fl(3, H, 8, hr),
            fl(3, H, group, 8, hr),
            fl(H, 8, hr),
            fl(H, n, 8, hr),
            fl(n, H, 8, hr),
            square,
            bf(wr, width),
            bf(n, th, width),
            bf(th, width),
            bf(n, th, width),
            fl(n * toks, 128),
            bf(th, width),
            bf(n, th, width),
            bf(n, th, width),
            fl(th, width),
            bf(groups, gr, width),
            bf(groups, gr, width),
            bf(groups, gr, width),
            bf(2, groups, gr, half),
            bf(groups, gr, half),
            bf(2, toks, half),
            bf(n, 2, toks, half),
            bf(toks, half),
            bf(n, toks, half),
            bf(n, toks, half),
            fl(toks, half),
            fl(8, toks),
            fl(2 * n, 8, toks),
            bf(wr, width),
            bf(wr, width),
            sems(2, nz),
            sems(4, H, n),
            sems(3, H, n),
            sems(3, H),
            sems(3, H, group),
            sems(H, n),
            sems(2, nz),
            sems(H),
            sems(n),
            sems(nz),
            sems(nz),
            sems(7),
            sems(4, n),
            sems(2, groups),
            sems(H, n),
            sems(2 * n),
        ],
        compiler_params=pltpu.CompilerParams(
            collective_id=0, has_side_effects=True, vmem_limit_bytes=62 * 2**20
        ),
    )(*operands)


def shards(
    noise,
    gen_gain,
    gen_weight,
    routes,
    critic_noise,
    critic_steps,
    crit_mod,
    crit_first,
    crit_second,
):
    width = noise.shape[1]
    groups = lax.axis_size(DP)
    x, y, z, role = (lax.axis_index(a) for a in (X, Y, Z, R))
    blocks_here = noise.shape[0] // BT
    most = 2 * blocks_here // groups

    modulation = crit_mod[0]
    mod_one = columns_of(modulation[0], x, width)[None, :]
    mod_two = columns_of(modulation[1], y, width)[None, :]
    gain_y = columns_of(gen_gain, y, width)[None, :]
    rows = critic_noise.shape[0]
    level = jnp.repeat(critic_steps.astype(F32) / levels, BT).reshape(H, 1, rows // H)
    level = jnp.broadcast_to(level, (H, 8, rows // H))

    me_index = y * lax.axis_size(Z) + z
    table = routes[:, 0]
    target_index = lax.dynamic_slice_in_dim(table, me_index * blocks_here, blocks_here, 0)
    order = jnp.arange(blocks_here, dtype=jnp.int32)
    earlier = (target_index[:, None] == target_index[None, :]) & (order[None, :] < order[:, None])
    rank = jnp.sum(earlier.astype(jnp.int32), axis=1)
    first_row = (target_index * most + rank) * BT
    row_of_token = (first_row[:, None] + jnp.arange(BT, dtype=jnp.int32)).reshape(-1)
    place_back = (row_of_token[:, None] == jnp.arange(rows, dtype=jnp.int32)[None, :]).astype(BF16)
    mine = row_of_token.reshape(2, -1)
    mine = jnp.where(role == 1, mine[1], mine[0])
    place = (jnp.arange(rows, dtype=jnp.int32)[:, None] == mine[None, :]).astype(BF16)
    counts = jnp.sum((table.reshape(groups, blocks_here) == me_index).astype(jnp.int32), axis=1)
    filled = (jnp.arange(most, dtype=jnp.int32)[None, :] < counts[:, None]).astype(F32)
    valid = jnp.repeat(filled.reshape(groups * most), BT)[:, None] / TOK_DEV

    noise_grad, grad_one, grad_two = step(
        lax.axis_size(X),
        lax.axis_size(Z),
        noise,
        gain_y,
        gen_weight,
        place,
        place_back,
        critic_noise,
        level,
        jnp.broadcast_to(valid, (rows, 128)),
        mod_one,
        mod_two,
        crit_first[0],
        crit_second[0],
    )
    return (noise_grad.reshape(-1, 1, 1, width // 2), grad_one[None], grad_two[None])


def solution(mesh):
    split = Mesh(
        mesh.devices.reshape(mesh.shape[R], mesh.shape[Y], -1, mesh.shape[Y]),
        (R, X, Z, Y),
    )
    in_specs = (
        P(DP, Y),
        P(),
        P(DP, Y),
        P(),
        P(DP, Y),
        P(DP),
        P(R, None, None),
        P(R, DP, Y),
        P(R, DP, Y),
    )
    out_specs = (P(DP, Y, R, None), P(R, DP, Y), P(R, DP, Y))
    return jax.shard_map(
        shards, mesh=split, in_specs=in_specs, out_specs=out_specs, check_vma=False
    )
```

```python
import functools

import jax
import jax.numpy as jnp
from jax import lax
from jax.experimental import pallas as pl
from jax.experimental.pallas import tpu as pltpu
from jax.sharding import Mesh
from jax.sharding import PartitionSpec as P

D = 3072
TOK_DEV = 128
BT = 4
R, X, Z, Y = "role", "dp_0", "dp_1", "mp"
DP = (X, Z)
YZ = (Y, Z)
F32, BF16 = jnp.float32, jnp.bfloat16

epsilon = 1e-06
levels = 1000.0


def columns_of(array, index, width):
    return lax.dynamic_slice_in_dim(array, index * width, width, array.ndim - 1)


H = 2
STEP = 32
MESH = pl.DeviceIdType.MESH


def sigmoid(v):
    return 1.0 / (1.0 + jnp.exp(-v))


def step_kernel(
    n,
    nz,
    noise,
    gain,
    wg_shard,
    place,
    place_back,
    cnoise_p,
    level_rows,
    valid,
    mod_one,
    mod_two,
    w1_shard,
    w2_shard,
    noise_grad,
    grad_one,
    grad_two,
    w1,
    w2,
    noisy_all,
    first_all,
    hidden_all,
    second_all,
    delta_all,
    up_all,
    root_q,
    root_p,
    level,
    clean,
    cnoise,
    pred,
    pred_other,
    swap_buf,
    part_out,
    part_in,
    own,
    g1_out,
    g1_in,
    g2_out,
    g2_in,
    column,
    stat_out,
    stat_in,
    inner_out,
    inner_in,
    level_in,
    wg,
    w2_mine,
    noise_in,
    noise_swap,
    gen_act,
    root_g,
    gen_made,
    gen_out,
    gen_in,
    gen_own,
    clean_out,
    clean_in,
    clean_other,
    gap,
    back_in,
    returned,
    ret_all,
    ret_swap,
    back_out,
    back_parts,
    back_own,
    gen_inner_out,
    gen_inner_in,
    g2_mine,
    g2_swap,
    w_sem,
    ag_sem,
    rs_sem,
    swap_sem,
    stat_sem,
    inner_sem,
    g_sem,
    role_sem,
    level_sem,
    wg_sem,
    wg_role_sem,
    one_sem,
    gen_sem,
    all_sem,
    noisy_sem,
    gen_inner_sem,
):
    r, x, z, y = (lax.axis_index(a) for a in (R, X, Z, Y))
    rows, width = cnoise.shape
    hr = rows // H
    wr = w1_shard.shape[0]
    toks = noise.shape[0]
    th = toks // 2
    half = width // 2
    groups = n * nz
    lanes = width // 128
    group = n * n
    here = x * n + y

    def dev(role=r, at_x=x, at_z=z, at_y=y):
        return (role, at_x, at_z, at_y)

    def remote(src, dst, sems, index, to):
        return pltpu.make_async_remote_copy(
            src_ref=src,
            dst_ref=dst,
            send_sem=sems.at[(0, *index)],
            recv_sem=sems.at[(1, *index)],
            device_id=to,
            device_id_type=MESH,
        )

    sent = []

    def each(low, high, body):
        def step(k, carry):
            body(k)
            return carry

        lax.fori_loop(low, high, step, 0)

    def wide(narrow):
        return jnp.concatenate([narrow] * lanes, axis=1)

    def cut(ref, start, count):
        return ref.at[pl.ds(pl.multiple_of(start, 16), count), :]

    barrier = pltpu.get_barrier_semaphore()

    def greet(to):
        pl.semaphore_signal(barrier, inc=1, device_id=to, device_id_type=MESH)

    def at(index):
        index = lax.rem(index, group)
        return index // n, lax.rem(index, n)

    def greet_plane(k):
        ax, ay = at(here + k)
        greet(dev(at_x=ax, at_y=ay))

    def greet_z(k):
        az = lax.rem(z + k, nz)
        greet(dev(at_x=y, at_z=az, at_y=x))

    my_yz = y * nz + z

    def yz(index):
        index = lax.rem(index, groups)
        return index // nz, lax.rem(index, nz)

    def greet_yz(k):
        ay, az = yz(my_yz + k)
        greet(dev(at_y=ay, at_z=az))

    each(1, group, greet_plane)
    each(1, nz, greet_z)
    each(1, groups, greet_yz)
    each(0, n, lambda k: greet(dev(role=1 - r, at_y=lax.rem(y + k, n))))
    pl.semaphore_wait(barrier, group - 1 + nz - 1 + groups - 1 + n)

    wh = wr // 2
    other = dev(role=1 - r)

    def wg_piece(source, role):
        return cut(wg, source * wr + role * wh, wh)

    def wg_copy(k):
        to = dev(at_x=y, at_z=z, at_y=x) if k is None else dev(at_z=lax.rem(z + k, nz))
        src = cut(wg_shard, r * wh, wh) if k is None else wg_piece(z, r)
        return remote(src, wg_piece(z, r), wg_sem, (0 if k is None else k,), to)

    def swapping(copy, src, dst):
        @pl.when(x != y)
        def _():
            copy.start()

        @pl.when(x == y)
        def _():
            dst[...] = src[...]

    swapping(wg_copy(None), cut(wg_shard, r * wh, wh), wg_piece(z, r))
    noise_mine = cut(noise, r * th, th)

    def noise_copy(k):
        to = dev(at_x=lax.rem(x + k, n))
        return remote(noise_mine, noise_in.at[x], gen_sem, (0, k), to)

    for k in range(1, n):
        noise_copy(k).start()
    across = dev(at_x=y, at_y=x)
    noise_swap_copy = remote(noise_mine, noise_swap, one_sem, (0,), across)
    swapping(noise_swap_copy, noise_mine, noise_swap)

    def row0(h, part):
        return h * (n * hr) + part * hr

    def gather_send(phase, h, buf, axis):
        me = x if axis == X else y
        for k in range(1, n):
            to = lax.rem(me + k, n)
            to = dev(at_x=to) if axis == X else dev(at_y=to)
            piece = cut(buf, row0(h, me), hr)
            copy = remote(piece, piece, ag_sem, (phase, h, k), to)
            copy.start()
            sent.append(copy)

    def gather_wait(phase, h, buf, axis):
        me = x if axis == X else y
        for k in range(1, n):
            piece = cut(buf, row0(h, lax.rem(me + n - k, n)), hr)
            remote(piece, piece, ag_sem, (phase, h, k), dev()).wait_recv()

    def swap_send(phase, h, src):
        dst = swap_buf.at[phase, h]

        @pl.when(x != y)
        def _():
            remote(src, dst, swap_sem, (phase, h), dev(at_x=y, at_y=x)).start()

        @pl.when(x == y)
        def _():
            dst[...] = src[...]

    def swap_wait(phase, h):
        dst = swap_buf.at[phase, h]

        @pl.when(x != y)
        def _():
            remote(dst, dst, swap_sem, (phase, h), dev(at_x=y, at_y=x)).wait_recv()

    def swap_sent(phase, h):
        dst = swap_buf.at[phase, h]

        @pl.when(x != y)
        def _():
            remote(dst, dst, swap_sem, (phase, h), dev(at_x=y, at_y=x)).wait_send()

    def stat_send(phase, h):
        summed = column[...].T[0:8, :]
        stat_out[phase, h] = summed
        stat_in[phase, h, here] = summed

        def send(k):
            ax, ay = at(here + k)
            remote(
                stat_out.at[phase, h],
                stat_in.at[phase, h, here],
                stat_sem,
                (phase, h, k),
                dev(at_x=ax, at_y=ay),
            ).start()

        each(1, group, send)

    def stat_wait(phase, h, root_ref):
        def wait(k):
            source = lax.rem(here + group - k, group)
            piece = stat_in.at[phase, h, source]
            remote(piece, piece, stat_sem, (phase, h, k), dev()).wait_recv()

        each(1, group, wait)
        for part in range(n):
            start = part * hr if phase == 2 else row0(h, part)
            total = stat_in[phase, h, part * n if phase else part]
            for c in range(1, n):
                index = part * n + c if phase else c * n + part
                total = total + stat_in[phase, h, index]
            root = lax.rsqrt(total / D + epsilon)
            root_ref[pl.ds(start, hr), :] = jnp.broadcast_to(root[0:1, :], (128, hr)).T

    def act_rows(src, dst, root_ref, mod, start):
        for i in range(0, hr, STEP):
            at_rows = pl.ds(pl.multiple_of(start + i, 16), STEP)
            scale = 1.0 + wide(level[at_rows, :]) * mod[...]
            shaped = src[at_rows, :].astype(F32) * wide(root_ref[at_rows, :]) * scale
            dst[at_rows, :] = (shaped / (1.0 + jnp.exp(-shaped))).astype(BF16)

    def layer(phase, h, axis, term):
        me = x if axis == X else y

        def one(k):
            part = lax.rem(me + k, n)
            start = row0(h, part)
            piece = cut(part_out.at[phase], start, hr)
            piece[...] = term(start).astype(BF16)
            to = dev(at_x=part) if axis == X else dev(at_y=part)
            remote(piece, part_in.at[phase, h, k], rs_sem, (phase, h, k), to).start()

        each(1, n, one)
        own[phase, h] = term(row0(h, me))

    def layer_wait(phase, h):
        for k in range(1, n):
            piece = part_in.at[phase, h, k]
            remote(piece, piece, rs_sem, (phase, h, k), dev()).wait_recv()

    def layer_sum(phase, h, i):
        total = own[phase, h, pl.ds(i, STEP), :]
        for k in range(1, n):
            total = total + part_in[phase, h, k, pl.ds(i, STEP), :].astype(F32)
        return total

    def dot(a, b, over_a, over_b):
        return lax.dot_general(
            a, b, (((over_a,), (over_b,)), ((), ())), preferred_element_type=F32
        )

    def sums(i, value):
        total = jnp.sum(value, axis=1, keepdims=True)
        column[pl.ds(i, STEP), :] = jnp.broadcast_to(total, (STEP, 128))

    def wg_role(source):
        return remote(
            wg_piece(source, r), wg_piece(source, r), wg_role_sem, (source,), other
        )

    def arrived(copy):
        @pl.when(x != y)
        def _():
            copy.wait_recv()

    arrived(wg_copy(None))
    each(1, nz, lambda k: wg_copy(k).start())
    wg_role(z).start()

    for i in range(0, toks, STEP):
        value = noise[pl.ds(i, STEP), :].astype(F32)
        sums(i, value * value)
    stat_send(2, 0)

    w1[pl.ds(pl.multiple_of(z * wr, 16), wr), :] = w1_shard[...]

    def w1_copy(k):
        to = lax.rem(z + k, nz)
        return remote(w1_shard, cut(w1, z * wr, wr), w_sem, (0, k), dev(at_z=to))

    def w2_copy(k):
        to = lax.rem(z + k, nz)
        return remote(w2_mine, cut(w2, z * wr, wr), w_sem, (1, k), dev(at_z=to))

    def w_wait(which, full):
        def wait(k):
            piece = cut(full, lax.rem(z + nz - k, nz) * wr, wr)
            remote(piece, piece, w_sem, (which, k), dev()).wait_recv()

        each(1, nz, wait)

    def level_copy(k):
        to = dev(at_x=lax.rem(x + k, n))
        return remote(level_rows, level_in.at[x], level_sem, (k,), to)

    for k in range(1, n):
        level_copy(k).start()
    level_in[x] = level_rows[...]
    w2_swap = remote(w2_shard, w2_mine, one_sem, (1,), across)
    swapping(w2_swap, w2_shard, w2_mine)
    half_rows = rows // 2
    cnoise_mine = cut(cnoise, r * half_rows, half_rows)
    cnoise_swap = remote(cut(cnoise_p, r * half_rows, half_rows), cnoise_mine, one_sem, (2,), across)
    swapping(cnoise_swap, cut(cnoise_p, r * half_rows, half_rows), cnoise_mine)
    cnoise_role = remote(cnoise_mine, cnoise_mine, one_sem, (7,), other)
    each(1, nz, lambda k: w1_copy(k).start())

    noise_in[x] = noise_mine[...]
    for k in range(1, n):
        piece = noise_in.at[lax.rem(x + n - k, n)]
        remote(piece, piece, gen_sem, (0, k), dev()).wait_recv()
    stat_wait(2, 0, root_g)

    def gen_rows(part):
        for i in range(0, th, STEP):
            at_rows = pl.ds(pl.multiple_of(part * toks + r * th + i, 16), STEP)
            shaped = noise_in[part, pl.ds(i, STEP), :].astype(F32) * wide(root_g[at_rows, :])
            shaped = shaped * gain[...]
            gen_act[part, pl.ds(i, STEP), :] = (shaped / (1.0 + jnp.exp(-shaped))).astype(BF16)

    each(0, n, gen_rows)

    def wg_on(k):
        source = lax.rem(z + nz - k, nz)
        piece = wg_piece(source, r)
        remote(piece, piece, wg_sem, (k,), dev()).wait_recv()
        wg_role(source).start()

    each(1, nz, wg_on)

    def wg_other(source):
        piece = wg_piece(source, 1 - r)
        remote(piece, piece, wg_role_sem, (source,), other).wait_recv()

    each(0, nz, wg_other)

    def gen_copy(k):
        part = lax.rem(y + k, n)
        return remote(gen_out.at[k], gen_in.at[k], gen_sem, (1, k), dev(at_y=part))

    def gen_part(k):
        part = lax.rem(y + k, n)
        gen_out[k] = dot(gen_act[part], wg[...], 1, 0).astype(BF16)
        gen_copy(k).start()

    each(1, n, gen_part)
    gen_own[...] = dot(gen_act[y], wg[...], 1, 0)
    for k in range(1, n):
        gen_copy(k).wait_recv()
    arrived(noise_swap_copy)
    for i in range(0, th, STEP):
        at_rows = pl.ds(i, STEP)
        total = noise_swap[at_rows, :].astype(F32) + gen_own[at_rows, :]
        for k in range(1, n):
            total = total + gen_in[k, at_rows, :].astype(F32)
        gen_made[at_rows, :] = total.astype(BF16)

    gr = rows // groups
    per = hr // gr
    for h in range(H):
        placed = dot(place[pl.ds(h * hr, hr), :], gen_made[...], 1, 0).astype(BF16)
        clean_out[pl.ds(h * per, per)] = placed.reshape(per, gr, width)

    def clean_copy(k):
        index = lax.rem(my_yz + k, groups)
        ay, az = yz(index)
        return remote(
            clean_out.at[index], clean_in.at[my_yz], all_sem, (0, k), dev(at_y=ay, at_z=az)
        )

    each(1, groups, lambda k: clean_copy(k).start())
    clean_in[my_yz] = clean_out[my_yz]

    arrived(w2_swap)
    w2[pl.ds(pl.multiple_of(z * wr, 16), wr), :] = w2_mine[...]
    each(1, nz, lambda k: w2_copy(k).start())
    for k in range(1, n):
        piece = level_in.at[lax.rem(x + n - k, n)]
        remote(piece, piece, level_sem, (k,), dev()).wait_recv()
    for h in range(H):
        for part in range(n):
            line = level_in[part, h]
            level[pl.ds(row0(h, part), hr), :] = jnp.broadcast_to(line[0:1, :], (128, hr)).T
    arrived(cnoise_swap)
    cnoise_role.start()
    cnoise_theirs = cut(cnoise, (1 - r) * half_rows, half_rows)
    remote(cnoise_theirs, cnoise_theirs, one_sem, (7,), other).wait_recv()

    def clean_wait(k):
        piece = clean_in.at[lax.rem(my_yz + groups - k, groups)]
        remote(piece, piece, all_sem, (0, k), dev()).wait_recv()

    each(1, groups, clean_wait)
    clean_role = remote(clean_in, clean_other, one_sem, (3,), other)
    clean_role.start()
    clean_role.wait_recv()

    rh = hr // 2

    def noisy_piece(h, part, role):
        return cut(noisy_all, row0(h, part) + role * rh, rh)

    def noisy_copy(h, k):
        piece = noisy_piece(h, y, r)
        return remote(piece, piece, ag_sem, (0, h, k), dev(at_y=lax.rem(y + k, n)))

    def noisy_role(h, k):
        piece = noisy_piece(h, lax.rem(y + n - k, n), r)
        return remote(piece, piece, noisy_sem, (h, k), other)

    for h in range(H):
        for i in range(0, hr, STEP):
            local = pl.ds(h * hr + i, STEP)
            if gr <= STEP:
                some = pl.ds((h * hr + i) // gr, STEP // gr)
                value = clean_in[some].astype(F32) + clean_other[some].astype(F32)
            else:
                some = (h * hr + i) // gr, pl.ds((h * hr + i) % gr, STEP)
                value = clean_in[some].astype(F32) + clean_other[some].astype(F32)
            value = value.reshape(STEP, width)
            clean[local, :] = value.astype(BF16)
            lev = wide(level[pl.ds(pl.multiple_of(row0(h, y) + i, 16), STEP), :])
            value = (1.0 - lev) * value + lev * cnoise[local, :].astype(F32)
            value = value.astype(BF16)
            noisy_all[pl.ds(pl.multiple_of(row0(h, y) + i, 16), STEP), :] = value
            value = value.astype(F32)
            sums(i, value * value)
        for k in range(1, n):
            noisy_copy(h, k).start()
        stat_send(0, h)

    def noisy_wait(h):
        for k in range(1, n):
            piece = noisy_piece(h, lax.rem(y + n - k, n), r)
            remote(piece, piece, ag_sem, (0, h, k), dev()).wait_recv()
            noisy_role(h, k).start()
        for k in range(1, n):
            piece = noisy_piece(h, lax.rem(y + n - k, n), 1 - r)
            remote(piece, piece, noisy_sem, (h, k), other).wait_recv()

    def residual(rows_all, start):
        return jnp.where(x == y, cut(rows_all, start, hr)[...].astype(F32), 0.0)

    for h in range(H):
        noisy_wait(h)
        stat_wait(0, h, root_q)
        each(0, n, lambda p, h=h: act_rows(noisy_all, first_all, root_q, mod_one, row0(h, p)))
        if h == 0:
            w_wait(0, w1)
        layer(
            0,
            h,
            X,
            lambda s: dot(cut(first_all, s, hr)[...], w1[...], 1, 0) + residual(noisy_all, s),
        )

    for h in range(H):
        layer_wait(0, h)
        for i in range(0, hr, STEP):
            value = layer_sum(0, h, i).astype(BF16)
            hidden_all[pl.ds(pl.multiple_of(row0(h, x) + i, 16), STEP), :] = value
            value = value.astype(F32)
            sums(i, value * value)
        gather_send(1, h, hidden_all, X)
        stat_send(1, h)

    for h in range(H):
        gather_wait(1, h, hidden_all, X)
        stat_wait(1, h, root_p)
        each(0, n, lambda p, h=h: act_rows(hidden_all, second_all, root_p, mod_two, row0(h, p)))
        if h == 0:
            w_wait(1, w2)
        layer(
            1,
            h,
            Y,
            lambda s: dot(cut(second_all, s, hr)[...], w2[...], 1, 0) + residual(hidden_all, s),
        )

    def role_copy(h):
        return remote(pred.at[h], pred_other.at[h], role_sem, (h,), dev(role=1 - r))

    for h in range(H):
        layer_wait(1, h)
        for i in range(0, hr, STEP):
            local = pl.ds(h * hr + i, STEP)
            value = layer_sum(1, h, i).astype(BF16)
            pred[h, pl.ds(i, STEP), :] = value
            target = cnoise[local, :].astype(F32) - clean[local, :].astype(F32)
            delta = ((value.astype(F32) - target) * wide(valid[local, :])).astype(BF16)
            delta_all[pl.ds(pl.multiple_of(row0(h, y) + i, 16), STEP), :] = delta
        gather_send(2, h, delta_all, Y)
        swap_send(0, h, cut(delta_all, row0(h, y), hr))
        role_copy(h).start()

    for h in range(H):
        gather_wait(2, h, delta_all, Y)
        layer(2, h, X, lambda s: dot(cut(delta_all, s, hr)[...], w2[...], 1, 1))

    def g_copy(which, out, into, block):
        return pltpu.make_async_remote_copy(
            src_ref=cut(out, block * wr, wr),
            dst_ref=into.at[z],
            send_sem=g_sem.at[0, which, block],
            recv_sem=g_sem.at[1, which, z],
            device_id=dev(at_z=block),
            device_id_type=MESH,
        )

    def g_term(which, left, right, out, into):
        for part in range(2):
            columns = pl.ds(part * half, half)
            for j in range(0, width, half):
                out[columns, pl.ds(j, half)] = dot(
                    left[:, columns], right[:, pl.ds(j, half)], 0, 0
                ).astype(BF16)

            def one(k, part=part):
                block = part * (nz // 2) + lax.rem(z + k, nz // 2)

                @pl.when(block != z)
                def _():
                    g_copy(which, out, into, block).start()

            each(0, nz // 2, one)
        into[z] = out[pl.ds(pl.multiple_of(z * wr, 16), wr), :]

    g_term(1, second_all, delta_all, g2_out, g2_in)

    for h in range(H):
        role_copy(h).wait_recv()
        for i in range(0, hr, max(STEP, gr)):
            count = max(STEP, gr)
            lev = wide(level[pl.ds(pl.multiple_of(row0(h, y) + i, 16), count), :])
            mine = pred[h, pl.ds(i, count), :].astype(F32)
            theirs = pred_other[h, pl.ds(i, count), :].astype(F32)
            diff = jnp.where(r == 1, mine - theirs, theirs - mine)
            diff = ((1.0 - lev) * diff).astype(BF16)
            some = pl.ds((h * hr + i) // gr, count // gr)
            for c in range(2):
                gap[c, some] = diff[:, c * half : (c + 1) * half].reshape(count // gr, gr, half)

    def back_copy(k):
        index = lax.rem(my_yz + k, groups)
        ay, az = yz(index)
        return remote(
            gap.at[r, index], back_in.at[my_yz], all_sem, (1, k), dev(at_y=ay, at_z=az)
        )

    each(1, groups, lambda k: back_copy(k).start())
    back_in[my_yz] = gap[r, my_yz]

    def norm_parts(h, i):
        at_rows = pl.ds(pl.multiple_of(row0(h, x) + i, 16), STEP)
        scale = 1.0 + wide(level[at_rows, :]) * mod_two[...]
        root = wide(root_p[at_rows, :])
        normed = hidden_all[at_rows, :].astype(F32) * root
        shaped = normed * scale
        sig = sigmoid(shaped)
        grad = layer_sum(2, h, i) * (sig * (1.0 + shaped * (1.0 - sig))) * scale
        return root, normed, grad

    def inner_copy(h, k):
        to = lax.rem(y + k, n)
        return remote(inner_out.at[h], inner_in.at[h, y], inner_sem, (h, k), dev(at_y=to))

    for h in range(H):
        layer_wait(2, h)
        for i in range(0, hr, STEP):
            _, normed, grad = norm_parts(h, i)
            own[0, h, pl.ds(i, STEP), :] = grad
            sums(i, grad * normed)
        inner_out[h] = column[...].T[0:8, :]
        inner_in[h, y] = inner_out[h]
        for k in range(1, n):
            inner_copy(h, k).start()

    for h in range(H):
        for k in range(1, n):
            piece = inner_in.at[h, lax.rem(y + n - k, n)]
            remote(piece, piece, inner_sem, (h, k), dev()).wait_recv()
        total = inner_in[h, 0]
        for c in range(1, n):
            total = total + inner_in[h, c]
        column[...] = jnp.broadcast_to(total[0:1, :] / D, (128, hr)).T
        swap_wait(0, h)
        for i in range(0, hr, STEP):
            at_rows = pl.ds(pl.multiple_of(row0(h, x) + i, 16), STEP)
            root = wide(root_p[at_rows, :])
            normed = hidden_all[at_rows, :].astype(F32) * root
            grad = own[0, h, pl.ds(i, STEP), :]
            back = root * (grad - normed * wide(column[pl.ds(i, STEP), :]))
            value = swap_buf[0, h, pl.ds(i, STEP), :].astype(F32) + back
            up_all[at_rows, :] = value.astype(BF16)
        gather_send(3, h, up_all, X)

    def back_wait(k):
        piece = back_in.at[lax.rem(my_yz + groups - k, groups)]
        remote(piece, piece, all_sem, (1, k), dev()).wait_recv()

    each(1, groups, back_wait)
    slots = back_in[...].reshape(rows, half)
    returned[r] = dot(place_back[...], slots, 1, 0).astype(BF16)
    ret_role = remote(returned.at[r], returned.at[r], one_sem, (4,), other)
    ret_role.start()
    ret_swap_copy = remote(returned.at[r], ret_swap, one_sem, (5,), across)
    swapping(ret_swap_copy, returned.at[r], ret_swap)
    theirs = returned.at[1 - r]
    remote(theirs, theirs, one_sem, (4,), other).wait_recv()
    ret_all[y] = returned[...]

    def ret_copy(k):
        return remote(returned, ret_all.at[y], gen_sem, (2, k), dev(at_y=lax.rem(y + k, n)))

    for k in range(1, n):
        ret_copy(k).start()

    for h in range(H):
        gather_wait(3, h, up_all, X)
    g_term(0, first_all, up_all, g1_out, g1_in)

    for k in range(1, n):
        piece = ret_all.at[lax.rem(y + n - k, n)]
        remote(piece, piece, gen_sem, (2, k), dev()).wait_recv()

    def back_part_copy(k):
        to = dev(at_x=lax.rem(x + k, n))
        return remote(back_out.at[k], back_parts.at[k], gen_sem, (3, k), to)

    def back_part(k):
        part = lax.rem(x + k, n)
        total = dot(ret_all[part, 0], weight_half(0), 1, 1)
        total = total + dot(ret_all[part, 1], weight_half(1), 1, 1)
        return total

    def weight_half(c):
        return wg[pl.ds(pl.multiple_of(r * half, 16), half), pl.ds(c * half, half)]

    def back_send(k):
        back_out[k] = back_part(k).astype(BF16)
        back_part_copy(k).start()

    each(1, n, back_send)
    back_own[...] = back_part(0)
    for k in range(1, n):
        back_part_copy(k).wait_recv()

    def my_half(ref, at_rows):
        low, high = ref[at_rows, pl.ds(0, half)], ref[at_rows, pl.ds(half, half)]
        return jnp.where(r == 1, high.astype(F32), low.astype(F32))

    def narrow(value):
        return jnp.concatenate([value] * (half // 128), axis=1)

    def gen_normed(i):
        at_rows = pl.ds(i, STEP)
        root = narrow(root_g[pl.ds(pl.multiple_of(x * toks + i, 16), STEP), :])
        return root, my_half(noise, at_rows) * root

    gain_half = my_half(gain, pl.ds(0, 1))
    for i in range(0, toks, STEP):
        at_rows = pl.ds(i, STEP)
        _, normed = gen_normed(i)
        shaped = normed * gain_half
        sig = sigmoid(shaped)
        total = back_own[at_rows, :]
        for k in range(1, n):
            total = total + back_parts[k, at_rows, :].astype(F32)
        grad = total * (sig * (1.0 + shaped * (1.0 - sig))) * gain_half
        back_own[at_rows, :] = grad
        sums(i, grad * normed)
    summed = column[...].T[0:8, :]
    gen_inner_out[...] = summed
    spot = r * n + y
    gen_inner_in[spot] = summed

    def gen_inner_copy(k):
        index = lax.rem(spot + k, 2 * n)
        to = dev(role=index // n, at_y=lax.rem(index, n))
        return remote(gen_inner_out, gen_inner_in.at[spot], gen_inner_sem, (k,), to)

    for k in range(1, 2 * n):
        gen_inner_copy(k).start()
    for k in range(1, 2 * n):
        piece = gen_inner_in.at[lax.rem(spot + 2 * n - k, 2 * n)]
        remote(piece, piece, gen_inner_sem, (k,), dev()).wait_recv()
    total = gen_inner_in[0]
    for c in range(1, 2 * n):
        total = total + gen_inner_in[c]
    column[...] = jnp.broadcast_to(total[0:1, :] / D, (128, toks)).T
    arrived(ret_swap_copy)
    for i in range(0, toks, STEP):
        at_rows = pl.ds(i, STEP)
        root, normed = gen_normed(i)
        back = root * (back_own[at_rows, :] - normed * narrow(column[at_rows, :]))
        noise_grad[at_rows, :] = ret_swap[at_rows, :].astype(F32) + back

    def g_finish(which, into, result):
        def wait(source):
            @pl.when(source != z)
            def _():
                piece = into.at[source]
                pltpu.make_async_remote_copy(
                    src_ref=piece,
                    dst_ref=piece,
                    send_sem=g_sem.at[0, which, source],
                    recv_sem=g_sem.at[1, which, source],
                    device_id=dev(),
                    device_id_type=MESH,
                ).wait_recv()

        each(0, nz, wait)
        for i in range(0, wr, STEP):
            total = into[0, pl.ds(i, STEP), :].astype(F32)
            for s in range(1, nz):
                total = total + into[s, pl.ds(i, STEP), :].astype(F32)
            result[pl.ds(i, STEP), :] = total.astype(result.dtype)

    g_finish(1, g2_in, g2_mine)
    g2_swap_copy = remote(g2_mine, g2_swap, one_sem, (6,), across)
    swapping(g2_swap_copy, g2_mine, g2_swap)
    g_finish(0, g1_in, grad_one)
    arrived(g2_swap_copy)
    grad_two[...] = g2_swap[...].astype(F32)

    def g_sent(which, out, into):
        def done(block):
            @pl.when(block != z)
            def _():
                g_copy(which, out, into, block).wait_send()

        each(0, nz, done)

    g_sent(1, g2_out, g2_in)
    g_sent(0, g1_out, g1_in)

    for copy in sent:
        copy.wait_send()
    each(1, nz, lambda k: w1_copy(k).wait_send())
    each(1, nz, lambda k: w2_copy(k).wait_send())

    each(1, nz, lambda k: wg_copy(k).wait_send())
    each(0, nz, lambda k: wg_role(k).wait_send())
    each(1, groups, lambda k: clean_copy(k).wait_send())
    each(1, groups, lambda k: back_copy(k).wait_send())
    clean_role.wait_send()
    cnoise_role.wait_send()
    ret_role.wait_send()
    each(1, group, lambda k: remote(
        stat_out.at[2, 0], stat_out.at[2, 0], stat_sem, (2, 0, k), dev()
    ).wait_send())

    @pl.when(x != y)
    def _():
        wg_copy(None).wait_send()
        for copy in (noise_swap_copy, w2_swap, cnoise_swap, ret_swap_copy, g2_swap_copy):
            copy.wait_send()

    for k in range(1, n):
        for copy in (noise_copy, level_copy, gen_copy, ret_copy, back_part_copy):
            copy(k).wait_send()
    for k in range(1, 2 * n):
        gen_inner_copy(k).wait_send()

    for h in range(H):
        role_copy(h).wait_send()
        for k in range(1, n):
            noisy_copy(h, k).wait_send()
            noisy_role(h, k).wait_send()
        swap_sent(0, h)
        for phase in range(3):
            def part_sent(k, phase=phase, h=h):
                piece = part_in.at[phase, h, k]
                remote(piece, piece, rs_sem, (phase, h, k), dev()).wait_send()

            each(1, n, part_sent)
        for phase in range(2):

            def stat_sent(k, phase=phase, h=h):
                piece = stat_out.at[phase, h]
                remote(piece, piece, stat_sem, (phase, h, k), dev()).wait_send()

            each(1, group, stat_sent)
        for k in range(1, n):
            inner_copy(h, k).wait_send()


def step(n, nz, *operands):
    noise, cnoise, w1_shard = operands[0], operands[5], operands[10]
    toks, width = noise.shape
    rows = cnoise.shape[0]
    hr, th, half = rows // H, toks // 2, width // 2
    wr = w1_shard.shape[0]
    group, groups = n * n, n * nz
    gr = rows // groups
    vmem = pl.BlockSpec(memory_space=pltpu.VMEM)
    bf = lambda *shape: pltpu.VMEM(shape, BF16)
    fl = lambda *shape: pltpu.VMEM(shape, F32)
    sems = lambda *shape: pltpu.SemaphoreType.DMA((2, *shape))
    whole = bf(n * rows, width)
    square = bf(nz * wr, width)
    pieces = bf(nz, wr, width)
    return pl.pallas_call(
        functools.partial(step_kernel, n, nz),
        out_shape=(
            jax.ShapeDtypeStruct((toks, half), F32),
            jax.ShapeDtypeStruct((wr, width), F32),
            jax.ShapeDtypeStruct((wr, width), F32),
        ),
        in_specs=[vmem] * 12,
        out_specs=(vmem,) * 3,
        scratch_shapes=[
            square,
            square,
            *[whole] * 6,
            fl(n * rows, 128),
            fl(n * rows, 128),
            fl(n * rows, 128),
            bf(rows, width),
            bf(rows, width),
            bf(H, hr, width),
            bf(H, hr, width),
            bf(1, H, hr, width),
            bf(3, n * rows, width),
            bf(3, H, n, hr, width),
            fl(3, H, hr, width),
            square,
            pieces,
            square,
            pieces,
            fl(hr, 128),
            fl(3, H, 8, hr),
            fl(3, H, group, 8, hr),
            fl(H, 8, hr),
            fl(H, n, 8, hr),
            fl(n, H, 8, hr),
            square,
            bf(wr, width),
            bf(n, th, width),
            bf(th, width),
            bf(n, th, width),
            fl(n * toks, 128),
            bf(th, width),
            bf(n, th, width),
            bf(n, th, width),
            fl(th, width),
            bf(groups, gr, width),
            bf(groups, gr, width),
            bf(groups, gr, width),
            bf(2, groups, gr, half),
            bf(groups, gr, half),
            bf(2, toks, half),
            bf(n, 2, toks, half),
            bf(toks, half),
            bf(n, toks, half),
            bf(n, toks, half),
            fl(toks, half),
            fl(8, toks),
            fl(2 * n, 8, toks),
            bf(wr, width),
            bf(wr, width),
            sems(2, nz),
            sems(4, H, n),
            sems(3, H, n),
            sems(1, H),
            sems(3, H, group),
            sems(H, n),
            sems(2, nz),
            sems(H),
            sems(n),
            sems(nz),
            sems(nz),
            sems(8),
            sems(4, n),
            sems(2, groups),
            sems(H, n),
            sems(2 * n),
        ],
        compiler_params=pltpu.CompilerParams(
            collective_id=0, has_side_effects=True, vmem_limit_bytes=62 * 2**20
        ),
    )(*operands)


def shards(
    noise,
    gen_gain,
    gen_weight,
    routes,
    critic_noise,
    critic_steps,
    crit_mod,
    crit_first,
    crit_second,
):
    width = noise.shape[1]
    groups = lax.axis_size(DP)
    x, y, z, role = (lax.axis_index(a) for a in (X, Y, Z, R))
    blocks_here = noise.shape[0] // BT
    most = 2 * blocks_here // groups

    modulation = crit_mod[0]
    mod_one = columns_of(modulation[0], x, width)[None, :]
    mod_two = columns_of(modulation[1], y, width)[None, :]
    gain_y = columns_of(gen_gain, y, width)[None, :]
    rows = critic_noise.shape[0]
    level = jnp.repeat(critic_steps.astype(F32) / levels, BT).reshape(H, 1, rows // H)
    level = jnp.broadcast_to(level, (H, 8, rows // H))

    me_index = y * lax.axis_size(Z) + z
    table = routes[:, 0]
    target_index = lax.dynamic_slice_in_dim(table, me_index * blocks_here, blocks_here, 0)
    order = jnp.arange(blocks_here, dtype=jnp.int32)
    earlier = (target_index[:, None] == target_index[None, :]) & (order[None, :] < order[:, None])
    rank = jnp.sum(earlier.astype(jnp.int32), axis=1)
    first_row = (target_index * most + rank) * BT
    row_of_token = (first_row[:, None] + jnp.arange(BT, dtype=jnp.int32)).reshape(-1)
    place_back = (row_of_token[:, None] == jnp.arange(rows, dtype=jnp.int32)[None, :]).astype(BF16)
    mine = row_of_token.reshape(2, -1)
    mine = jnp.where(role == 1, mine[1], mine[0])
    place = (jnp.arange(rows, dtype=jnp.int32)[:, None] == mine[None, :]).astype(BF16)
    counts = jnp.sum((table.reshape(groups, blocks_here) == me_index).astype(jnp.int32), axis=1)
    filled = (jnp.arange(most, dtype=jnp.int32)[None, :] < counts[:, None]).astype(F32)
    valid = jnp.repeat(filled.reshape(groups * most), BT)[:, None] / TOK_DEV

    noise_grad, grad_one, grad_two = step(
        lax.axis_size(X),
        lax.axis_size(Z),
        noise,
        gain_y,
        gen_weight,
        place,
        place_back,
        critic_noise,
        level,
        jnp.broadcast_to(valid, (rows, 128)),
        mod_one,
        mod_two,
        crit_first[0],
        crit_second[0],
    )
    return (noise_grad.reshape(-1, 1, 1, width // 2), grad_one[None], grad_two[None])


def solution(mesh):
    split = Mesh(
        mesh.devices.reshape(mesh.shape[R], mesh.shape[Y], -1, mesh.shape[Y]),
        (R, X, Z, Y),
    )
    in_specs = (
        P(DP, Y),
        P(),
        P(DP, Y),
        P(),
        P(DP, Y),
        P(DP),
        P(R, None, None),
        P(R, DP, Y),
        P(R, DP, Y),
    )
    out_specs = (P(DP, Y, R, None), P(R, DP, Y), P(R, DP, Y))
    return jax.shard_map(
        shards, mesh=split, in_specs=in_specs, out_specs=out_specs, check_vma=False
    )
```

```python
import functools

import jax
import jax.numpy as jnp
from jax import lax
from jax.experimental import pallas as pl
from jax.experimental.pallas import tpu as pltpu
from jax.sharding import Mesh
from jax.sharding import PartitionSpec as P

D = 3072
TOK_DEV = 128
BT = 4
R, X, Z, Y = "role", "dp_0", "dp_1", "mp"
DP = (X, Z)
YZ = (Y, Z)
F32, BF16 = jnp.float32, jnp.bfloat16

epsilon = 1e-06
levels = 1000.0


H = 2
STEP = 32
MESH = pl.DeviceIdType.MESH


def sigmoid(v):
    return 1.0 / (1.0 + jnp.exp(-v))


def step_kernel(
    n,
    nz,
    noise,
    gains,
    wg_shard,
    place,
    place_back,
    cnoise_p,
    level_rows,
    valid,
    mods,
    w1_shard,
    w2_shard,
    noise_grad,
    grad_one,
    grad_two,
    w1,
    w2,
    noisy_all,
    first_all,
    hidden_all,
    second_all,
    delta_all,
    up_all,
    root_q,
    root_p,
    level,
    clean,
    cnoise,
    pred,
    pred_other,
    swap_buf,
    part_out,
    part_in,
    own,
    g1_out,
    g1_in,
    g2_out,
    g2_in,
    column,
    stat_out,
    stat_in,
    inner_out,
    inner_in,
    level_in,
    wg,
    w2_mine,
    noise_in,
    noise_swap,
    gen_act,
    root_g,
    gen_made,
    gen_out,
    gen_in,
    gen_own,
    clean_out,
    clean_in,
    clean_other,
    gap,
    back_in,
    returned,
    ret_all,
    ret_swap,
    back_out,
    back_parts,
    back_own,
    gen_inner_out,
    gen_inner_in,
    g2_mine,
    g2_swap,
    w_sem,
    ag_sem,
    rs_sem,
    swap_sem,
    stat_sem,
    inner_sem,
    g_sem,
    role_sem,
    level_sem,
    wg_sem,
    wg_role_sem,
    one_sem,
    gen_sem,
    all_sem,
    noisy_sem,
    gen_inner_sem,
):
    r, x, z, y = (lax.axis_index(a) for a in (R, X, Z, Y))
    rows, width = cnoise.shape
    hr = rows // H
    wr = w1_shard.shape[0]

    def columns(ref, row, index):
        return ref.at[pl.ds(row, 1), pl.ds(pl.multiple_of(index * width, 128), width)]

    mod_one, mod_two, gain = columns(mods, 0, x), columns(mods, 1, y), columns(gains, 0, y)
    toks = noise.shape[0]
    th = toks // 2
    half = width // 2
    groups = n * nz
    lanes = width // 128
    group = n * n
    here = x * n + y

    def dev(role=r, at_x=x, at_z=z, at_y=y):
        return (role, at_x, at_z, at_y)

    def remote(src, dst, sems, index, to):
        return pltpu.make_async_remote_copy(
            src_ref=src,
            dst_ref=dst,
            send_sem=sems.at[(0, *index)],
            recv_sem=sems.at[(1, *index)],
            device_id=to,
            device_id_type=MESH,
        )

    sent = []

    def each(low, high, body):
        def step(k, carry):
            body(k)
            return carry

        lax.fori_loop(low, high, step, 0)

    def wide(narrow):
        return jnp.concatenate([narrow] * lanes, axis=1)

    def cut(ref, start, count):
        return ref.at[pl.ds(pl.multiple_of(start, 16), count), :]

    barrier = pltpu.get_barrier_semaphore()

    def greet(to):
        pl.semaphore_signal(barrier, inc=1, device_id=to, device_id_type=MESH)

    def at(index):
        index = lax.rem(index, group)
        return index // n, lax.rem(index, n)

    def greet_plane(k):
        ax, ay = at(here + k)
        greet(dev(at_x=ax, at_y=ay))

    def greet_z(k):
        az = lax.rem(z + k, nz)
        greet(dev(at_x=y, at_z=az, at_y=x))

    my_yz = y * nz + z

    def yz(index):
        index = lax.rem(index, groups)
        return index // nz, lax.rem(index, nz)

    def greet_yz(k):
        ay, az = yz(my_yz + k)
        greet(dev(at_y=ay, at_z=az))

    each(1, group, greet_plane)
    each(1, nz, greet_z)
    each(1, groups, greet_yz)
    each(0, n, lambda k: greet(dev(role=1 - r, at_y=lax.rem(y + k, n))))
    pl.semaphore_wait(barrier, group - 1 + nz - 1 + groups - 1 + n)

    wh = wr // 2
    other = dev(role=1 - r)

    def wg_piece(source, role):
        return cut(wg, source * wr + role * wh, wh)

    def wg_copy(k):
        to = dev(at_x=y, at_z=z, at_y=x) if k is None else dev(at_z=lax.rem(z + k, nz))
        src = cut(wg_shard, r * wh, wh) if k is None else wg_piece(z, r)
        return remote(src, wg_piece(z, r), wg_sem, (0 if k is None else k,), to)

    def swapping(copy, src, dst):
        @pl.when(x != y)
        def _():
            copy.start()

        @pl.when(x == y)
        def _():
            dst[...] = src[...]

    swapping(wg_copy(None), cut(wg_shard, r * wh, wh), wg_piece(z, r))
    noise_mine = cut(noise, r * th, th)

    def noise_copy(k):
        to = dev(at_x=lax.rem(x + k, n))
        return remote(noise_mine, noise_in.at[x], gen_sem, (0, k), to)

    for k in range(1, n):
        noise_copy(k).start()
    across = dev(at_x=y, at_y=x)
    noise_swap_copy = remote(noise_mine, noise_swap, one_sem, (0,), across)
    swapping(noise_swap_copy, noise_mine, noise_swap)

    def row0(h, part):
        return h * (n * hr) + part * hr

    def gather_send(phase, h, buf, axis):
        me = x if axis == X else y
        for k in range(1, n):
            to = lax.rem(me + k, n)
            to = dev(at_x=to) if axis == X else dev(at_y=to)
            piece = cut(buf, row0(h, me), hr)
            copy = remote(piece, piece, ag_sem, (phase, h, k), to)
            copy.start()
            sent.append(copy)

    def gather_wait(phase, h, buf, axis):
        me = x if axis == X else y
        for k in range(1, n):
            piece = cut(buf, row0(h, lax.rem(me + n - k, n)), hr)
            remote(piece, piece, ag_sem, (phase, h, k), dev()).wait_recv()

    far_part = lax.rem(y + n - x, n)
    stays = (x == y) & (far_part == x)

    def swap_copy(h):
        src = cut(delta_all, row0(h, far_part), hr)
        return remote(src, swap_buf.at[h], swap_sem, (h,), dev(at_x=far_part, at_y=x))

    def swap_send(h):
        @pl.when(jnp.logical_not(stays))
        def _():
            swap_copy(h).start()

        @pl.when(stays)
        def _():
            swap_buf[h] = cut(delta_all, row0(h, far_part), hr)[...]

    def swap_wait(h):
        @pl.when(jnp.logical_not(stays))
        def _():
            swap_copy(h).wait_recv()

    def swap_sent(h):
        @pl.when(jnp.logical_not(stays))
        def _():
            swap_copy(h).wait_send()

    def stat_send(phase, h):
        summed = column[...].T[0:8, :]
        stat_out[phase, h] = summed
        stat_in[phase, h, here] = summed

        def send(k):
            ax, ay = at(here + k)
            remote(
                stat_out.at[phase, h],
                stat_in.at[phase, h, here],
                stat_sem,
                (phase, h, k),
                dev(at_x=ax, at_y=ay),
            ).start()

        each(1, group, send)

    def stat_wait(phase, h, root_ref):
        def wait(k):
            source = lax.rem(here + group - k, group)
            piece = stat_in.at[phase, h, source]
            remote(piece, piece, stat_sem, (phase, h, k), dev()).wait_recv()

        each(1, group, wait)
        for part in range(n):
            start = part * hr if phase == 2 else row0(h, part)
            total = stat_in[phase, h, part * n if phase else part]
            for c in range(1, n):
                index = part * n + c if phase else c * n + part
                total = total + stat_in[phase, h, index]
            root = lax.rsqrt(total / D + epsilon)
            root_ref[pl.ds(start, hr), :] = jnp.broadcast_to(root[0:1, :], (128, hr)).T

    def act_rows(src, dst, root_ref, mod, start):
        for i in range(0, hr, STEP):
            at_rows = pl.ds(pl.multiple_of(start + i, 16), STEP)
            scale = 1.0 + wide(level[at_rows, :]) * mod[...]
            shaped = src[at_rows, :].astype(F32) * wide(root_ref[at_rows, :]) * scale
            dst[at_rows, :] = (shaped / (1.0 + jnp.exp(-shaped))).astype(BF16)

    def layer(phase, h, axis, term):
        me = x if axis == X else y

        def one(k):
            part = lax.rem(me + k, n)
            start = row0(h, part)
            piece = cut(part_out.at[phase], start, hr)
            piece[...] = term(start).astype(BF16)
            to = dev(at_x=part) if axis == X else dev(at_y=part)
            remote(piece, part_in.at[phase, h, k], rs_sem, (phase, h, k), to).start()

        each(1, n, one)
        own[phase, h] = term(row0(h, me))

    def layer_wait(phase, h):
        for k in range(1, n):
            piece = part_in.at[phase, h, k]
            remote(piece, piece, rs_sem, (phase, h, k), dev()).wait_recv()

    def layer_sum(phase, h, i):
        total = own[phase, h, pl.ds(i, STEP), :]
        for k in range(1, n):
            total = total + part_in[phase, h, k, pl.ds(i, STEP), :].astype(F32)
        return total

    def dot(a, b, over_a, over_b):
        return lax.dot_general(
            a, b, (((over_a,), (over_b,)), ((), ())), preferred_element_type=F32
        )

    def sums(i, value):
        total = jnp.sum(value, axis=1, keepdims=True)
        column[pl.ds(i, STEP), :] = jnp.broadcast_to(total, (STEP, 128))

    def wg_role(source):
        return remote(
            wg_piece(source, r), wg_piece(source, r), wg_role_sem, (source,), other
        )

    def arrived(copy):
        @pl.when(x != y)
        def _():
            copy.wait_recv()

    arrived(wg_copy(None))
    each(1, nz, lambda k: wg_copy(k).start())
    wg_role(z).start()

    for i in range(0, toks, STEP):
        value = noise[pl.ds(i, STEP), :].astype(F32)
        sums(i, value * value)
    stat_send(2, 0)

    w1[pl.ds(pl.multiple_of(z * wr, 16), wr), :] = w1_shard[...]

    def w1_copy(k):
        to = lax.rem(z + k, nz)
        return remote(w1_shard, cut(w1, z * wr, wr), w_sem, (0, k), dev(at_z=to))

    def w2_copy(k):
        to = lax.rem(z + k, nz)
        return remote(w2_mine, cut(w2, z * wr, wr), w_sem, (1, k), dev(at_z=to))

    def w_wait(which, full):
        def wait(k):
            piece = cut(full, lax.rem(z + nz - k, nz) * wr, wr)
            remote(piece, piece, w_sem, (which, k), dev()).wait_recv()

        each(1, nz, wait)

    def level_copy(k):
        to = dev(at_x=lax.rem(x + k, n))
        return remote(level_rows, level_in.at[x], level_sem, (k,), to)

    for k in range(1, n):
        level_copy(k).start()
    level_in[x] = level_rows[...]
    w2_swap = remote(w2_shard, w2_mine, one_sem, (1,), across)
    swapping(w2_swap, w2_shard, w2_mine)
    half_rows = rows // 2
    cnoise_mine = cut(cnoise, r * half_rows, half_rows)
    cnoise_swap = remote(cut(cnoise_p, r * half_rows, half_rows), cnoise_mine, one_sem, (2,), across)
    swapping(cnoise_swap, cut(cnoise_p, r * half_rows, half_rows), cnoise_mine)
    cnoise_role = remote(cnoise_mine, cnoise_mine, one_sem, (7,), other)
    each(1, nz, lambda k: w1_copy(k).start())

    noise_in[x] = noise_mine[...]
    for k in range(1, n):
        piece = noise_in.at[lax.rem(x + n - k, n)]
        remote(piece, piece, gen_sem, (0, k), dev()).wait_recv()
    stat_wait(2, 0, root_g)

    def gen_rows(part):
        for i in range(0, th, STEP):
            at_rows = pl.ds(pl.multiple_of(part * toks + r * th + i, 16), STEP)
            shaped = noise_in[part, pl.ds(i, STEP), :].astype(F32) * wide(root_g[at_rows, :])
            shaped = shaped * gain[...]
            gen_act[part, pl.ds(i, STEP), :] = (shaped / (1.0 + jnp.exp(-shaped))).astype(BF16)

    each(0, n, gen_rows)

    def wg_on(k):
        source = lax.rem(z + nz - k, nz)
        piece = wg_piece(source, r)
        remote(piece, piece, wg_sem, (k,), dev()).wait_recv()
        wg_role(source).start()

    each(1, nz, wg_on)

    def wg_other(source):
        piece = wg_piece(source, 1 - r)
        remote(piece, piece, wg_role_sem, (source,), other).wait_recv()

    each(0, nz, wg_other)

    def gen_copy(k):
        part = lax.rem(y + k, n)
        return remote(gen_out.at[k], gen_in.at[k], gen_sem, (1, k), dev(at_y=part))

    def gen_part(k):
        part = lax.rem(y + k, n)
        gen_out[k] = dot(gen_act[part], wg[...], 1, 0).astype(BF16)
        gen_copy(k).start()

    each(1, n, gen_part)
    gen_own[...] = dot(gen_act[y], wg[...], 1, 0)
    for k in range(1, n):
        gen_copy(k).wait_recv()
    arrived(noise_swap_copy)
    for i in range(0, th, STEP):
        at_rows = pl.ds(i, STEP)
        total = noise_swap[at_rows, :].astype(F32) + gen_own[at_rows, :]
        for k in range(1, n):
            total = total + gen_in[k, at_rows, :].astype(F32)
        gen_made[at_rows, :] = total.astype(BF16)

    gr = rows // groups
    per = hr // gr
    for h in range(H):
        placed = dot(place[pl.ds(h * hr, hr), :], gen_made[...], 1, 0).astype(BF16)
        clean_out[pl.ds(h * per, per)] = placed.reshape(per, gr, width)

    def clean_copy(k):
        index = lax.rem(my_yz + k, groups)
        ay, az = yz(index)
        return remote(
            clean_out.at[index], clean_in.at[my_yz], all_sem, (0, k), dev(at_y=ay, at_z=az)
        )

    each(1, groups, lambda k: clean_copy(k).start())
    clean_in[my_yz] = clean_out[my_yz]

    arrived(w2_swap)
    w2[pl.ds(pl.multiple_of(z * wr, 16), wr), :] = w2_mine[...]
    each(1, nz, lambda k: w2_copy(k).start())
    for k in range(1, n):
        piece = level_in.at[lax.rem(x + n - k, n)]
        remote(piece, piece, level_sem, (k,), dev()).wait_recv()
    for h in range(H):
        for part in range(n):
            line = level_in[part, h]
            level[pl.ds(row0(h, part), hr), :] = jnp.broadcast_to(line[0:1, :], (128, hr)).T
    arrived(cnoise_swap)
    cnoise_role.start()
    cnoise_theirs = cut(cnoise, (1 - r) * half_rows, half_rows)
    remote(cnoise_theirs, cnoise_theirs, one_sem, (7,), other).wait_recv()

    def clean_wait(k):
        piece = clean_in.at[lax.rem(my_yz + groups - k, groups)]
        remote(piece, piece, all_sem, (0, k), dev()).wait_recv()

    each(1, groups, clean_wait)
    clean_role = remote(clean_in, clean_other, one_sem, (3,), other)
    clean_role.start()
    clean_role.wait_recv()

    rh = hr // 2

    def noisy_piece(h, part, role):
        return cut(noisy_all, row0(h, part) + role * rh, rh)

    def noisy_copy(h, k):
        piece = noisy_piece(h, y, r)
        return remote(piece, piece, ag_sem, (0, h, k), dev(at_y=lax.rem(y + k, n)))

    def noisy_role(h, k):
        piece = noisy_piece(h, lax.rem(y + n - k, n), r)
        return remote(piece, piece, noisy_sem, (h, k), other)

    for h in range(H):
        for i in range(0, hr, STEP):
            local = pl.ds(h * hr + i, STEP)
            if gr <= STEP:
                some = pl.ds((h * hr + i) // gr, STEP // gr)
                value = clean_in[some].astype(F32) + clean_other[some].astype(F32)
            else:
                some = (h * hr + i) // gr, pl.ds((h * hr + i) % gr, STEP)
                value = clean_in[some].astype(F32) + clean_other[some].astype(F32)
            value = value.reshape(STEP, width)
            clean[local, :] = value.astype(BF16)
            lev = wide(level[pl.ds(pl.multiple_of(row0(h, y) + i, 16), STEP), :])
            value = (1.0 - lev) * value + lev * cnoise[local, :].astype(F32)
            value = value.astype(BF16)
            noisy_all[pl.ds(pl.multiple_of(row0(h, y) + i, 16), STEP), :] = value
            value = value.astype(F32)
            sums(i, value * value)
        for k in range(1, n):
            noisy_copy(h, k).start()
        stat_send(0, h)

    def noisy_wait(h):
        for k in range(1, n):
            piece = noisy_piece(h, lax.rem(y + n - k, n), r)
            remote(piece, piece, ag_sem, (0, h, k), dev()).wait_recv()
            noisy_role(h, k).start()
        for k in range(1, n):
            piece = noisy_piece(h, lax.rem(y + n - k, n), 1 - r)
            remote(piece, piece, noisy_sem, (h, k), other).wait_recv()

    def residual(rows_all, start):
        return jnp.where(x == y, cut(rows_all, start, hr)[...].astype(F32), 0.0)

    for h in range(H):
        noisy_wait(h)
        stat_wait(0, h, root_q)
        each(0, n, lambda p, h=h: act_rows(noisy_all, first_all, root_q, mod_one, row0(h, p)))
        if h == 0:
            w_wait(0, w1)
        layer(
            0,
            h,
            X,
            lambda s: dot(cut(first_all, s, hr)[...], w1[...], 1, 0) + residual(noisy_all, s),
        )

    for h in range(H):
        layer_wait(0, h)
        for i in range(0, hr, STEP):
            value = layer_sum(0, h, i).astype(BF16)
            hidden_all[pl.ds(pl.multiple_of(row0(h, x) + i, 16), STEP), :] = value
            value = value.astype(F32)
            sums(i, value * value)
        gather_send(1, h, hidden_all, X)
        stat_send(1, h)

    for h in range(H):
        gather_wait(1, h, hidden_all, X)
        stat_wait(1, h, root_p)
        each(0, n, lambda p, h=h: act_rows(hidden_all, second_all, root_p, mod_two, row0(h, p)))
        if h == 0:
            w_wait(1, w2)
        layer(
            1,
            h,
            Y,
            lambda s: dot(cut(second_all, s, hr)[...], w2[...], 1, 0) + residual(hidden_all, s),
        )

    def role_copy(h):
        return remote(pred.at[h], pred_other.at[h], role_sem, (h,), dev(role=1 - r))

    for h in range(H):
        layer_wait(1, h)
        for i in range(0, hr, STEP):
            local = pl.ds(h * hr + i, STEP)
            value = layer_sum(1, h, i).astype(BF16)
            pred[h, pl.ds(i, STEP), :] = value
            target = cnoise[local, :].astype(F32) - clean[local, :].astype(F32)
            delta = ((value.astype(F32) - target) * wide(valid[local, :])).astype(BF16)
            delta_all[pl.ds(pl.multiple_of(row0(h, y) + i, 16), STEP), :] = delta
        gather_send(2, h, delta_all, Y)
        role_copy(h).start()

    for h in range(H):
        gather_wait(2, h, delta_all, Y)
        swap_send(h)
        layer(2, h, X, lambda s: dot(cut(delta_all, s, hr)[...], w2[...], 1, 1))

    def g_copy(which, out, into, block):
        return pltpu.make_async_remote_copy(
            src_ref=cut(out, block * wr, wr),
            dst_ref=into.at[z],
            send_sem=g_sem.at[0, which, block],
            recv_sem=g_sem.at[1, which, z],
            device_id=dev(at_z=block),
            device_id_type=MESH,
        )

    def g_term(which, left, right, out, into):
        for part in range(2):
            columns = pl.ds(part * half, half)
            for j in range(0, width, half):
                out[columns, pl.ds(j, half)] = dot(
                    left[:, columns], right[:, pl.ds(j, half)], 0, 0
                ).astype(BF16)

            def one(k, part=part):
                block = part * (nz // 2) + lax.rem(z + k, nz // 2)

                @pl.when(block != z)
                def _():
                    g_copy(which, out, into, block).start()

            each(0, nz // 2, one)
        into[z] = out[pl.ds(pl.multiple_of(z * wr, 16), wr), :]

    g_term(1, second_all, delta_all, g2_out, g2_in)

    for h in range(H):
        role_copy(h).wait_recv()
        for i in range(0, hr, max(STEP, gr)):
            count = max(STEP, gr)
            lev = wide(level[pl.ds(pl.multiple_of(row0(h, y) + i, 16), count), :])
            mine = pred[h, pl.ds(i, count), :].astype(F32)
            theirs = pred_other[h, pl.ds(i, count), :].astype(F32)
            diff = jnp.where(r == 1, mine - theirs, theirs - mine)
            diff = ((1.0 - lev) * diff).astype(BF16)
            some = pl.ds((h * hr + i) // gr, count // gr)
            for c in range(2):
                gap[c, some] = diff[:, c * half : (c + 1) * half].reshape(count // gr, gr, half)

    def back_copy(k):
        index = lax.rem(my_yz + k, groups)
        ay, az = yz(index)
        return remote(
            gap.at[r, index], back_in.at[my_yz], all_sem, (1, k), dev(at_y=ay, at_z=az)
        )

    each(1, groups, lambda k: back_copy(k).start())
    back_in[my_yz] = gap[r, my_yz]

    def norm_parts(h, i):
        at_rows = pl.ds(pl.multiple_of(row0(h, x) + i, 16), STEP)
        scale = 1.0 + wide(level[at_rows, :]) * mod_two[...]
        root = wide(root_p[at_rows, :])
        normed = hidden_all[at_rows, :].astype(F32) * root
        shaped = normed * scale
        sig = sigmoid(shaped)
        grad = layer_sum(2, h, i) * (sig * (1.0 + shaped * (1.0 - sig))) * scale
        return root, normed, grad

    def inner_copy(h, k):
        to = lax.rem(y + k, n)
        return remote(inner_out.at[h], inner_in.at[h, y], inner_sem, (h, k), dev(at_y=to))

    for h in range(H):
        layer_wait(2, h)
        for i in range(0, hr, STEP):
            _, normed, grad = norm_parts(h, i)
            own[0, h, pl.ds(i, STEP), :] = grad
            sums(i, grad * normed)
        inner_out[h] = column[...].T[0:8, :]
        inner_in[h, y] = inner_out[h]
        for k in range(1, n):
            inner_copy(h, k).start()

    for h in range(H):
        for k in range(1, n):
            piece = inner_in.at[h, lax.rem(y + n - k, n)]
            remote(piece, piece, inner_sem, (h, k), dev()).wait_recv()
        total = inner_in[h, 0]
        for c in range(1, n):
            total = total + inner_in[h, c]
        column[...] = jnp.broadcast_to(total[0:1, :] / D, (128, hr)).T
        swap_wait(h)
        for i in range(0, hr, STEP):
            at_rows = pl.ds(pl.multiple_of(row0(h, x) + i, 16), STEP)
            root = wide(root_p[at_rows, :])
            normed = hidden_all[at_rows, :].astype(F32) * root
            grad = own[0, h, pl.ds(i, STEP), :]
            back = root * (grad - normed * wide(column[pl.ds(i, STEP), :]))
            value = swap_buf[h, pl.ds(i, STEP), :].astype(F32) + back
            up_all[at_rows, :] = value.astype(BF16)
        gather_send(3, h, up_all, X)

    def back_wait(k):
        piece = back_in.at[lax.rem(my_yz + groups - k, groups)]
        remote(piece, piece, all_sem, (1, k), dev()).wait_recv()

    each(1, groups, back_wait)
    slots = back_in[...].reshape(rows, half)
    returned[r] = dot(place_back[...], slots, 1, 0).astype(BF16)
    ret_role = remote(returned.at[r], returned.at[r], one_sem, (4,), other)
    ret_role.start()
    ret_swap_copy = remote(returned.at[r], ret_swap, one_sem, (5,), across)
    swapping(ret_swap_copy, returned.at[r], ret_swap)
    theirs = returned.at[1 - r]
    remote(theirs, theirs, one_sem, (4,), other).wait_recv()
    ret_all[y] = returned[...]

    def ret_copy(k):
        return remote(returned, ret_all.at[y], gen_sem, (2, k), dev(at_y=lax.rem(y + k, n)))

    for k in range(1, n):
        ret_copy(k).start()

    for h in range(H):
        gather_wait(3, h, up_all, X)
    g_term(0, first_all, up_all, g1_out, g1_in)

    for k in range(1, n):
        piece = ret_all.at[lax.rem(y + n - k, n)]
        remote(piece, piece, gen_sem, (2, k), dev()).wait_recv()

    def back_part_copy(k):
        to = dev(at_x=lax.rem(x + k, n))
        return remote(back_out.at[k], back_parts.at[k], gen_sem, (3, k), to)

    def back_part(k):
        part = lax.rem(x + k, n)
        total = dot(ret_all[part, 0], weight_half(0), 1, 1)
        total = total + dot(ret_all[part, 1], weight_half(1), 1, 1)
        return total

    def weight_half(c):
        return wg[pl.ds(pl.multiple_of(r * half, 16), half), pl.ds(c * half, half)]

    def back_send(k):
        back_out[k] = back_part(k).astype(BF16)
        back_part_copy(k).start()

    each(1, n, back_send)
    back_own[...] = back_part(0)
    for k in range(1, n):
        back_part_copy(k).wait_recv()

    def my_half(ref, at_rows):
        low, high = ref[at_rows, pl.ds(0, half)], ref[at_rows, pl.ds(half, half)]
        return jnp.where(r == 1, high.astype(F32), low.astype(F32))

    def narrow(value):
        return jnp.concatenate([value] * (half // 128), axis=1)

    def gen_normed(i):
        at_rows = pl.ds(i, STEP)
        root = narrow(root_g[pl.ds(pl.multiple_of(x * toks + i, 16), STEP), :])
        return root, my_half(noise, at_rows) * root

    gain_half = my_half(gain, pl.ds(0, 1))
    for i in range(0, toks, STEP):
        at_rows = pl.ds(i, STEP)
        _, normed = gen_normed(i)
        shaped = normed * gain_half
        sig = sigmoid(shaped)
        total = back_own[at_rows, :]
        for k in range(1, n):
            total = total + back_parts[k, at_rows, :].astype(F32)
        grad = total * (sig * (1.0 + shaped * (1.0 - sig))) * gain_half
        back_own[at_rows, :] = grad
        sums(i, grad * normed)
    summed = column[...].T[0:8, :]
    gen_inner_out[...] = summed
    spot = r * n + y
    gen_inner_in[spot] = summed

    def gen_inner_copy(k):
        index = lax.rem(spot + k, 2 * n)
        to = dev(role=index // n, at_y=lax.rem(index, n))
        return remote(gen_inner_out, gen_inner_in.at[spot], gen_inner_sem, (k,), to)

    for k in range(1, 2 * n):
        gen_inner_copy(k).start()
    for k in range(1, 2 * n):
        piece = gen_inner_in.at[lax.rem(spot + 2 * n - k, 2 * n)]
        remote(piece, piece, gen_inner_sem, (k,), dev()).wait_recv()
    total = gen_inner_in[0]
    for c in range(1, 2 * n):
        total = total + gen_inner_in[c]
    column[...] = jnp.broadcast_to(total[0:1, :] / D, (128, toks)).T
    arrived(ret_swap_copy)
    for i in range(0, toks, STEP):
        at_rows = pl.ds(i, STEP)
        root, normed = gen_normed(i)
        back = root * (back_own[at_rows, :] - normed * narrow(column[at_rows, :]))
        noise_grad[at_rows, :] = ret_swap[at_rows, :].astype(F32) + back

    def g_finish(which, into, result):
        def wait(source):
            @pl.when(source != z)
            def _():
                piece = into.at[source]
                pltpu.make_async_remote_copy(
                    src_ref=piece,
                    dst_ref=piece,
                    send_sem=g_sem.at[0, which, source],
                    recv_sem=g_sem.at[1, which, source],
                    device_id=dev(),
                    device_id_type=MESH,
                ).wait_recv()

        each(0, nz, wait)
        for i in range(0, wr, STEP):
            total = into[0, pl.ds(i, STEP), :].astype(F32)
            for s in range(1, nz):
                total = total + into[s, pl.ds(i, STEP), :].astype(F32)
            result[pl.ds(i, STEP), :] = total.astype(result.dtype)

    g_finish(1, g2_in, g2_mine)
    g2_swap_copy = remote(g2_mine, g2_swap, one_sem, (6,), across)
    swapping(g2_swap_copy, g2_mine, g2_swap)
    g_finish(0, g1_in, grad_one)
    arrived(g2_swap_copy)
    grad_two[...] = g2_swap[...].astype(F32)

    def g_sent(which, out, into):
        def done(block):
            @pl.when(block != z)
            def _():
                g_copy(which, out, into, block).wait_send()

        each(0, nz, done)

    g_sent(1, g2_out, g2_in)
    g_sent(0, g1_out, g1_in)

    for copy in sent:
        copy.wait_send()
    each(1, nz, lambda k: w1_copy(k).wait_send())
    each(1, nz, lambda k: w2_copy(k).wait_send())

    each(1, nz, lambda k: wg_copy(k).wait_send())
    each(0, nz, lambda k: wg_role(k).wait_send())
    each(1, groups, lambda k: clean_copy(k).wait_send())
    each(1, groups, lambda k: back_copy(k).wait_send())
    clean_role.wait_send()
    cnoise_role.wait_send()
    ret_role.wait_send()
    each(1, group, lambda k: remote(
        stat_out.at[2, 0], stat_out.at[2, 0], stat_sem, (2, 0, k), dev()
    ).wait_send())

    @pl.when(x != y)
    def _():
        wg_copy(None).wait_send()
        for copy in (noise_swap_copy, w2_swap, cnoise_swap, ret_swap_copy, g2_swap_copy):
            copy.wait_send()

    for k in range(1, n):
        for copy in (noise_copy, level_copy, gen_copy, ret_copy, back_part_copy):
            copy(k).wait_send()
    for k in range(1, 2 * n):
        gen_inner_copy(k).wait_send()

    for h in range(H):
        role_copy(h).wait_send()
        for k in range(1, n):
            noisy_copy(h, k).wait_send()
            noisy_role(h, k).wait_send()
        swap_sent(h)
        for phase in range(3):
            def part_sent(k, phase=phase, h=h):
                piece = part_in.at[phase, h, k]
                remote(piece, piece, rs_sem, (phase, h, k), dev()).wait_send()

            each(1, n, part_sent)
        for phase in range(2):

            def stat_sent(k, phase=phase, h=h):
                piece = stat_out.at[phase, h]
                remote(piece, piece, stat_sem, (phase, h, k), dev()).wait_send()

            each(1, group, stat_sent)
        for k in range(1, n):
            inner_copy(h, k).wait_send()


def step(n, nz, *operands):
    noise, cnoise, w1_shard = operands[0], operands[5], operands[9]
    toks, width = noise.shape
    rows = cnoise.shape[0]
    hr, th, half = rows // H, toks // 2, width // 2
    wr = w1_shard.shape[0]
    group, groups = n * n, n * nz
    gr = rows // groups
    vmem = pl.BlockSpec(memory_space=pltpu.VMEM)
    bf = lambda *shape: pltpu.VMEM(shape, BF16)
    fl = lambda *shape: pltpu.VMEM(shape, F32)
    sems = lambda *shape: pltpu.SemaphoreType.DMA((2, *shape))
    whole = bf(n * rows, width)
    square = bf(nz * wr, width)
    pieces = bf(nz, wr, width)
    return pl.pallas_call(
        functools.partial(step_kernel, n, nz),
        out_shape=(
            jax.ShapeDtypeStruct((toks, half), F32),
            jax.ShapeDtypeStruct((wr, width), F32),
            jax.ShapeDtypeStruct((wr, width), F32),
        ),
        in_specs=[vmem] * 11,
        out_specs=(vmem,) * 3,
        scratch_shapes=[
            square,
            square,
            *[whole] * 6,
            fl(n * rows, 128),
            fl(n * rows, 128),
            fl(n * rows, 128),
            bf(rows, width),
            bf(rows, width),
            bf(H, hr, width),
            bf(H, hr, width),
            bf(H, hr, width),
            bf(3, n * rows, width),
            bf(3, H, n, hr, width),
            fl(3, H, hr, width),
            square,
            pieces,
            square,
            pieces,
            fl(hr, 128),
            fl(3, H, 8, hr),
            fl(3, H, group, 8, hr),
            fl(H, 8, hr),
            fl(H, n, 8, hr),
            fl(n, H, 8, hr),
            square,
            bf(wr, width),
            bf(n, th, width),
            bf(th, width),
            bf(n, th, width),
            fl(n * toks, 128),
            bf(th, width),
            bf(n, th, width),
            bf(n, th, width),
            fl(th, width),
            bf(groups, gr, width),
            bf(groups, gr, width),
            bf(groups, gr, width),
            bf(2, groups, gr, half),
            bf(groups, gr, half),
            bf(2, toks, half),
            bf(n, 2, toks, half),
            bf(toks, half),
            bf(n, toks, half),
            bf(n, toks, half),
            fl(toks, half),
            fl(8, toks),
            fl(2 * n, 8, toks),
            bf(wr, width),
            bf(wr, width),
            sems(2, nz),
            sems(4, H, n),
            sems(3, H, n),
            sems(H),
            sems(3, H, group),
            sems(H, n),
            sems(2, nz),
            sems(H),
            sems(n),
            sems(nz),
            sems(nz),
            sems(8),
            sems(4, n),
            sems(2, groups),
            sems(H, n),
            sems(2 * n),
        ],
        compiler_params=pltpu.CompilerParams(
            collective_id=0, has_side_effects=True, vmem_limit_bytes=62 * 2**20
        ),
    )(*operands)


def shards(
    noise,
    gen_gain,
    gen_weight,
    routes,
    critic_noise,
    critic_steps,
    crit_mod,
    crit_first,
    crit_second,
):
    width = noise.shape[1]
    groups = lax.axis_size(DP)
    x, y, z, role = (lax.axis_index(a) for a in (X, Y, Z, R))
    blocks_here = noise.shape[0] // BT
    most = 2 * blocks_here // groups

    rows = critic_noise.shape[0]
    level = jnp.repeat(critic_steps.astype(F32) / levels, BT).reshape(H, 1, rows // H)
    level = jnp.broadcast_to(level, (H, 8, rows // H))

    me_index = y * lax.axis_size(Z) + z
    table = routes[:, 0]
    target_index = lax.dynamic_slice_in_dim(table, me_index * blocks_here, blocks_here, 0)
    order = jnp.arange(blocks_here, dtype=jnp.int32)
    earlier = (target_index[:, None] == target_index[None, :]) & (order[None, :] < order[:, None])
    rank = jnp.sum(earlier.astype(jnp.int32), axis=1)
    first_row = (target_index * most + rank) * BT
    row_of_token = (first_row[:, None] + jnp.arange(BT, dtype=jnp.int32)).reshape(-1)
    place_back = (row_of_token[:, None] == jnp.arange(rows, dtype=jnp.int32)[None, :]).astype(BF16)
    mine = row_of_token.reshape(2, -1)
    mine = jnp.where(role == 1, mine[1], mine[0])
    place = (jnp.arange(rows, dtype=jnp.int32)[:, None] == mine[None, :]).astype(BF16)
    counts = jnp.sum((table.reshape(groups, blocks_here) == me_index).astype(jnp.int32), axis=1)
    filled = (jnp.arange(most, dtype=jnp.int32)[None, :] < counts[:, None]).astype(F32)
    valid = jnp.repeat(filled.reshape(groups * most), BT)[:, None] / TOK_DEV

    noise_grad, grad_one, grad_two = step(
        lax.axis_size(X),
        lax.axis_size(Z),
        noise,
        gen_gain[None, :],
        gen_weight,
        place,
        place_back,
        critic_noise,
        level,
        jnp.broadcast_to(valid, (rows, 128)),
        crit_mod[0],
        crit_first[0],
        crit_second[0],
    )
    return (noise_grad.reshape(-1, 1, 1, width // 2), grad_one[None], grad_two[None])


def solution(mesh):
    split = Mesh(
        mesh.devices.reshape(mesh.shape[R], mesh.shape[Y], -1, mesh.shape[Y]),
        (R, X, Z, Y),
    )
    in_specs = (
        P(DP, Y),
        P(),
        P(DP, Y),
        P(),
        P(DP, Y),
        P(DP),
        P(R, None, None),
        P(R, DP, Y),
        P(R, DP, Y),
    )
    out_specs = (P(DP, Y, R, None), P(R, DP, Y), P(R, DP, Y))
    return jax.shard_map(
        shards, mesh=split, in_specs=in_specs, out_specs=out_specs, check_vma=False
    )
```

```python
import functools

import jax
import jax.numpy as jnp
from jax import lax
from jax.experimental import pallas as pl
from jax.experimental.pallas import tpu as pltpu
from jax.sharding import Mesh
from jax.sharding import PartitionSpec as P

D = 3072
TOK_DEV = 128
BT = 4
R, X, Z, Y = "role", "dp_0", "dp_1", "mp"
DP = (X, Z)
YZ = (Y, Z)
F32, BF16 = jnp.float32, jnp.bfloat16

epsilon = 1e-06
levels = 1000.0


H = 2
STEP = 32
MESH = pl.DeviceIdType.MESH


def sigmoid(v):
    return 1.0 / (1.0 + jnp.exp(-v))


def step_kernel(
    n,
    nz,
    noise,
    gains,
    wg_shard,
    place,
    place_back,
    cnoise_p,
    level_rows,
    valid,
    mods,
    w1_shard,
    w2_shard,
    noise_grad,
    grad_one,
    grad_two,
    w1,
    w2,
    noisy_all,
    first_all,
    hidden_all,
    second_all,
    delta_all,
    up_all,
    root_q,
    root_p,
    level,
    clean,
    cnoise,
    pred,
    pred_other,
    swap_buf,
    part_out,
    part_in,
    own,
    g1_out,
    g1_in,
    g2_out,
    g2_in,
    column,
    stat_out,
    stat_in,
    inner_out,
    inner_in,
    level_in,
    wg,
    w2_mine,
    noise_in,
    noise_swap,
    gen_act,
    root_g,
    gen_made,
    gen_out,
    gen_in,
    gen_own,
    clean_out,
    clean_in,
    clean_other,
    gap,
    back_in,
    returned,
    ret_all,
    ret_swap,
    back_out,
    back_parts,
    back_own,
    gen_inner_out,
    gen_inner_in,
    g2_mine,
    g2_swap,
    w_sem,
    ag_sem,
    rs_sem,
    swap_sem,
    stat_sem,
    inner_sem,
    g_sem,
    role_sem,
    level_sem,
    wg_sem,
    wg_role_sem,
    one_sem,
    gen_sem,
    all_sem,
    noisy_sem,
    gen_inner_sem,
):
    r, x, z, y = (lax.axis_index(a) for a in (R, X, Z, Y))
    rows, width = cnoise.shape
    hr = rows // H
    wr = w1_shard.shape[0]

    def columns(ref, row, index):
        return ref.at[pl.ds(row, 1), pl.ds(pl.multiple_of(index * width, 128), width)]

    mod_one, mod_two, gain = columns(mods, 0, x), columns(mods, 1, y), columns(gains, 0, y)
    toks = noise.shape[0]
    th = toks // 2
    half = width // 2
    groups = n * nz
    lanes = width // 128
    group = n * n
    here = x * n + y

    def dev(role=r, at_x=x, at_z=z, at_y=y):
        return (role, at_x, at_z, at_y)

    def remote(src, dst, sems, index, to):
        return pltpu.make_async_remote_copy(
            src_ref=src,
            dst_ref=dst,
            send_sem=sems.at[(0, *index)],
            recv_sem=sems.at[(1, *index)],
            device_id=to,
            device_id_type=MESH,
        )

    sent = []

    def each(low, high, body):
        def step(k, carry):
            body(k)
            return carry

        lax.fori_loop(low, high, step, 0)

    def wide(narrow):
        return jnp.concatenate([narrow] * lanes, axis=1)

    def cut(ref, start, count):
        return ref.at[pl.ds(pl.multiple_of(start, 16), count), :]

    barrier = pltpu.get_barrier_semaphore()

    def greet(to):
        pl.semaphore_signal(barrier, inc=1, device_id=to, device_id_type=MESH)

    def at(index):
        index = lax.rem(index, group)
        return index // n, lax.rem(index, n)

    def greet_plane(k):
        ax, ay = at(here + k)
        greet(dev(at_x=ax, at_y=ay))

    def greet_z(k):
        az = lax.rem(z + k, nz)
        greet(dev(at_x=y, at_z=az, at_y=x))

    my_yz = y * nz + z

    def yz(index):
        index = lax.rem(index, groups)
        return index // nz, lax.rem(index, nz)

    def greet_yz(k):
        ay, az = yz(my_yz + k)
        greet(dev(at_y=ay, at_z=az))

    each(1, group, greet_plane)
    each(1, nz, greet_z)
    each(1, groups, greet_yz)
    each(0, n, lambda k: greet(dev(role=1 - r, at_y=lax.rem(y + k, n))))
    pl.semaphore_wait(barrier, group - 1 + nz - 1 + groups - 1 + n)

    wh = wr // 2
    other = dev(role=1 - r)

    def wg_piece(source, role):
        return cut(wg, source * wr + role * wh, wh)

    def wg_copy(k):
        to = dev(at_x=y, at_z=z, at_y=x) if k is None else dev(at_z=lax.rem(z + k, nz))
        src = cut(wg_shard, r * wh, wh) if k is None else wg_piece(z, r)
        return remote(src, wg_piece(z, r), wg_sem, (0 if k is None else k,), to)

    def swapping(copy, src, dst):
        @pl.when(x != y)
        def _():
            copy.start()

        @pl.when(x == y)
        def _():
            dst[...] = src[...]

    swapping(wg_copy(None), cut(wg_shard, r * wh, wh), wg_piece(z, r))
    noise_mine = cut(noise, r * th, th)

    def noise_copy(k):
        to = dev(at_x=lax.rem(x + k, n))
        return remote(noise_mine, noise_in.at[x], gen_sem, (0, k), to)

    for k in range(1, n):
        noise_copy(k).start()
    across = dev(at_x=y, at_y=x)
    noise_swap_copy = remote(noise_mine, noise_swap, one_sem, (0,), across)
    swapping(noise_swap_copy, noise_mine, noise_swap)

    def row0(h, part):
        return h * (n * hr) + part * hr

    def gather_send(phase, h, buf, axis):
        me = x if axis == X else y
        for k in range(1, n):
            to = lax.rem(me + k, n)
            to = dev(at_x=to) if axis == X else dev(at_y=to)
            piece = cut(buf, row0(h, me), hr)
            copy = remote(piece, piece, ag_sem, (phase, h, k), to)
            copy.start()
            sent.append(copy)

    def gather_wait(phase, h, buf, axis):
        me = x if axis == X else y
        for k in range(1, n):
            piece = cut(buf, row0(h, lax.rem(me + n - k, n)), hr)
            remote(piece, piece, ag_sem, (phase, h, k), dev()).wait_recv()

    far_part = lax.rem(y + n - x, n)
    stays = (x == y) & (far_part == x)

    def swap_copy(h):
        src = cut(delta_all, row0(h, far_part), hr)
        return remote(src, swap_buf.at[h], swap_sem, (h,), dev(at_x=far_part, at_y=x))

    def swap_send(h):
        @pl.when(jnp.logical_not(stays))
        def _():
            swap_copy(h).start()

        @pl.when(stays)
        def _():
            swap_buf[h] = cut(delta_all, row0(h, far_part), hr)[...]

    def swap_wait(h):
        @pl.when(jnp.logical_not(stays))
        def _():
            swap_copy(h).wait_recv()

    def swap_sent(h):
        @pl.when(jnp.logical_not(stays))
        def _():
            swap_copy(h).wait_send()

    def stat_send(phase, h):
        summed = column[...].T[0:8, :]
        stat_out[phase, h] = summed
        stat_in[phase, h, here] = summed

        def send(k):
            ax, ay = at(here + k)
            remote(
                stat_out.at[phase, h],
                stat_in.at[phase, h, here],
                stat_sem,
                (phase, h, k),
                dev(at_x=ax, at_y=ay),
            ).start()

        each(1, group, send)

    def stat_wait(phase, h, root_ref):
        def wait(k):
            source = lax.rem(here + group - k, group)
            piece = stat_in.at[phase, h, source]
            remote(piece, piece, stat_sem, (phase, h, k), dev()).wait_recv()

        each(1, group, wait)
        for part in range(n):
            start = part * hr if phase == 2 else row0(h, part)
            total = stat_in[phase, h, part * n if phase else part]
            for c in range(1, n):
                index = part * n + c if phase else c * n + part
                total = total + stat_in[phase, h, index]
            root = lax.rsqrt(total / D + epsilon)
            root_ref[pl.ds(start, hr), :] = jnp.broadcast_to(root[0:1, :], (128, hr)).T

    def act_rows(src, dst, root_ref, mod, start):
        for i in range(0, hr, STEP):
            at_rows = pl.ds(pl.multiple_of(start + i, 16), STEP)
            scale = 1.0 + wide(level[at_rows, :]) * mod[...]
            shaped = src[at_rows, :].astype(F32) * wide(root_ref[at_rows, :]) * scale
            dst[at_rows, :] = (shaped / (1.0 + jnp.exp(-shaped))).astype(BF16)

    def layer(phase, h, axis, term):
        me = x if axis == X else y

        def one(k):
            part = lax.rem(me + k, n)
            start = row0(h, part)
            piece = cut(part_out.at[phase], start, hr)
            piece[...] = term(start).astype(BF16)
            to = dev(at_x=part) if axis == X else dev(at_y=part)
            remote(piece, part_in.at[phase, h, k], rs_sem, (phase, h, k), to).start()

        each(1, n, one)
        own[phase, h] = term(row0(h, me))

    def layer_wait(phase, h):
        for k in range(1, n):
            piece = part_in.at[phase, h, k]
            remote(piece, piece, rs_sem, (phase, h, k), dev()).wait_recv()

    def layer_sum(phase, h, i):
        total = own[phase, h, pl.ds(i, STEP), :]
        for k in range(1, n):
            total = total + part_in[phase, h, k, pl.ds(i, STEP), :].astype(F32)
        return total

    def dot(a, b, over_a, over_b):
        return lax.dot_general(
            a, b, (((over_a,), (over_b,)), ((), ())), preferred_element_type=F32
        )

    def sums(i, value):
        total = jnp.sum(value, axis=1, keepdims=True)
        column[pl.ds(i, STEP), :] = jnp.broadcast_to(total, (STEP, 128))

    def wg_role(source):
        return remote(
            wg_piece(source, r), wg_piece(source, r), wg_role_sem, (source,), other
        )

    def arrived(copy):
        @pl.when(x != y)
        def _():
            copy.wait_recv()

    arrived(wg_copy(None))
    each(1, nz, lambda k: wg_copy(k).start())
    wg_role(z).start()

    for i in range(0, toks, STEP):
        value = noise[pl.ds(i, STEP), :].astype(F32)
        sums(i, value * value)
    stat_send(2, 0)

    w1[pl.ds(pl.multiple_of(z * wr, 16), wr), :] = w1_shard[...]

    def w1_copy(k):
        to = lax.rem(z + k, nz)
        return remote(w1_shard, cut(w1, z * wr, wr), w_sem, (0, k), dev(at_z=to))

    def w2_copy(k):
        to = lax.rem(z + k, nz)
        return remote(w2_mine, cut(w2, z * wr, wr), w_sem, (1, k), dev(at_z=to))

    def w_wait(which, full):
        def wait(k):
            piece = cut(full, lax.rem(z + nz - k, nz) * wr, wr)
            remote(piece, piece, w_sem, (which, k), dev()).wait_recv()

        each(1, nz, wait)

    def level_copy(k):
        to = dev(at_x=lax.rem(x + k, n))
        return remote(level_rows, level_in.at[x], level_sem, (k,), to)

    for k in range(1, n):
        level_copy(k).start()
    level_in[x] = level_rows[...]
    w2_swap = remote(w2_shard, w2_mine, one_sem, (1,), across)
    half_rows = rows // 2
    cnoise_mine = cut(cnoise, r * half_rows, half_rows)
    cnoise_swap = remote(cut(cnoise_p, r * half_rows, half_rows), cnoise_mine, one_sem, (2,), across)
    cnoise_role = remote(cnoise_mine, cnoise_mine, one_sem, (7,), other)
    each(1, nz, lambda k: w1_copy(k).start())

    noise_in[x] = noise_mine[...]
    for k in range(1, n):
        piece = noise_in.at[lax.rem(x + n - k, n)]
        remote(piece, piece, gen_sem, (0, k), dev()).wait_recv()
    swapping(cnoise_swap, cut(cnoise_p, r * half_rows, half_rows), cnoise_mine)
    stat_wait(2, 0, root_g)

    def gen_rows(part):
        for i in range(0, th, STEP):
            at_rows = pl.ds(pl.multiple_of(part * toks + r * th + i, 16), STEP)
            shaped = noise_in[part, pl.ds(i, STEP), :].astype(F32) * wide(root_g[at_rows, :])
            shaped = shaped * gain[...]
            gen_act[part, pl.ds(i, STEP), :] = (shaped / (1.0 + jnp.exp(-shaped))).astype(BF16)

    each(0, n, gen_rows)

    def wg_on(k):
        source = lax.rem(z + nz - k, nz)
        piece = wg_piece(source, r)
        remote(piece, piece, wg_sem, (k,), dev()).wait_recv()
        wg_role(source).start()

    each(1, nz, wg_on)

    def wg_other(source):
        piece = wg_piece(source, 1 - r)
        remote(piece, piece, wg_role_sem, (source,), other).wait_recv()

    each(0, nz, wg_other)

    def gen_copy(k):
        part = lax.rem(y + k, n)
        return remote(gen_out.at[k], gen_in.at[k], gen_sem, (1, k), dev(at_y=part))

    def gen_part(k):
        part = lax.rem(y + k, n)
        gen_out[k] = dot(gen_act[part], wg[...], 1, 0).astype(BF16)
        gen_copy(k).start()

    each(1, n, gen_part)
    gen_own[...] = dot(gen_act[y], wg[...], 1, 0)
    for k in range(1, n):
        gen_copy(k).wait_recv()
    arrived(noise_swap_copy)
    for i in range(0, th, STEP):
        at_rows = pl.ds(i, STEP)
        total = noise_swap[at_rows, :].astype(F32) + gen_own[at_rows, :]
        for k in range(1, n):
            total = total + gen_in[k, at_rows, :].astype(F32)
        gen_made[at_rows, :] = total.astype(BF16)

    gr = rows // groups
    per = hr // gr
    for h in range(H):
        placed = dot(place[pl.ds(h * hr, hr), :], gen_made[...], 1, 0).astype(BF16)
        clean_out[pl.ds(h * per, per)] = placed.reshape(per, gr, width)

    def clean_copy(k):
        index = lax.rem(my_yz + k, groups)
        ay, az = yz(index)
        return remote(
            clean_out.at[index], clean_in.at[my_yz], all_sem, (0, k), dev(at_y=ay, at_z=az)
        )

    each(1, groups, lambda k: clean_copy(k).start())
    clean_in[my_yz] = clean_out[my_yz]

    swapping(w2_swap, w2_shard, w2_mine)
    for k in range(1, n):
        piece = level_in.at[lax.rem(x + n - k, n)]
        remote(piece, piece, level_sem, (k,), dev()).wait_recv()
    for h in range(H):
        for part in range(n):
            line = level_in[part, h]
            level[pl.ds(row0(h, part), hr), :] = jnp.broadcast_to(line[0:1, :], (128, hr)).T
    arrived(cnoise_swap)
    cnoise_role.start()
    cnoise_theirs = cut(cnoise, (1 - r) * half_rows, half_rows)
    remote(cnoise_theirs, cnoise_theirs, one_sem, (7,), other).wait_recv()

    def clean_wait(k):
        piece = clean_in.at[lax.rem(my_yz + groups - k, groups)]
        remote(piece, piece, all_sem, (0, k), dev()).wait_recv()

    each(1, groups, clean_wait)
    clean_role = remote(clean_in, clean_other, one_sem, (3,), other)
    clean_role.start()
    clean_role.wait_recv()

    rh = hr // 2

    def noisy_piece(h, part, role):
        return cut(noisy_all, row0(h, part) + role * rh, rh)

    def noisy_copy(h, k):
        piece = noisy_piece(h, y, r)
        return remote(piece, piece, ag_sem, (0, h, k), dev(at_y=lax.rem(y + k, n)))

    def noisy_role(h, k):
        piece = noisy_piece(h, lax.rem(y + n - k, n), r)
        return remote(piece, piece, noisy_sem, (h, k), other)

    for h in range(H):
        for i in range(0, hr, STEP):
            local = pl.ds(h * hr + i, STEP)
            if gr <= STEP:
                some = pl.ds((h * hr + i) // gr, STEP // gr)
                value = clean_in[some].astype(F32) + clean_other[some].astype(F32)
            else:
                some = (h * hr + i) // gr, pl.ds((h * hr + i) % gr, STEP)
                value = clean_in[some].astype(F32) + clean_other[some].astype(F32)
            value = value.reshape(STEP, width)
            clean[local, :] = value.astype(BF16)
            lev = wide(level[pl.ds(pl.multiple_of(row0(h, y) + i, 16), STEP), :])
            value = (1.0 - lev) * value + lev * cnoise[local, :].astype(F32)
            value = value.astype(BF16)
            noisy_all[pl.ds(pl.multiple_of(row0(h, y) + i, 16), STEP), :] = value
            value = value.astype(F32)
            sums(i, value * value)
        for k in range(1, n):
            noisy_copy(h, k).start()
        stat_send(0, h)

    arrived(w2_swap)
    w2[pl.ds(pl.multiple_of(z * wr, 16), wr), :] = w2_mine[...]
    each(1, nz, lambda k: w2_copy(k).start())

    def noisy_wait(h):
        for k in range(1, n):
            piece = noisy_piece(h, lax.rem(y + n - k, n), r)
            remote(piece, piece, ag_sem, (0, h, k), dev()).wait_recv()
            noisy_role(h, k).start()
        for k in range(1, n):
            piece = noisy_piece(h, lax.rem(y + n - k, n), 1 - r)
            remote(piece, piece, noisy_sem, (h, k), other).wait_recv()

    def residual(rows_all, start):
        return jnp.where(x == y, cut(rows_all, start, hr)[...].astype(F32), 0.0)

    for h in range(H):
        noisy_wait(h)
        stat_wait(0, h, root_q)
        each(0, n, lambda p, h=h: act_rows(noisy_all, first_all, root_q, mod_one, row0(h, p)))
        if h == 0:
            w_wait(0, w1)
        layer(
            0,
            h,
            X,
            lambda s: dot(cut(first_all, s, hr)[...], w1[...], 1, 0) + residual(noisy_all, s),
        )

    for h in range(H):
        layer_wait(0, h)
        for i in range(0, hr, STEP):
            value = layer_sum(0, h, i).astype(BF16)
            hidden_all[pl.ds(pl.multiple_of(row0(h, x) + i, 16), STEP), :] = value
            value = value.astype(F32)
            sums(i, value * value)
        gather_send(1, h, hidden_all, X)
        stat_send(1, h)

    for h in range(H):
        gather_wait(1, h, hidden_all, X)
        stat_wait(1, h, root_p)
        each(0, n, lambda p, h=h: act_rows(hidden_all, second_all, root_p, mod_two, row0(h, p)))
        if h == 0:
            w_wait(1, w2)
        layer(
            1,
            h,
            Y,
            lambda s: dot(cut(second_all, s, hr)[...], w2[...], 1, 0) + residual(hidden_all, s),
        )

    def role_copy(h):
        return remote(pred.at[h], pred_other.at[h], role_sem, (h,), dev(role=1 - r))

    for h in range(H):
        layer_wait(1, h)
        for i in range(0, hr, STEP):
            local = pl.ds(h * hr + i, STEP)
            value = layer_sum(1, h, i).astype(BF16)
            pred[h, pl.ds(i, STEP), :] = value
            target = cnoise[local, :].astype(F32) - clean[local, :].astype(F32)
            delta = ((value.astype(F32) - target) * wide(valid[local, :])).astype(BF16)
            delta_all[pl.ds(pl.multiple_of(row0(h, y) + i, 16), STEP), :] = delta
        gather_send(2, h, delta_all, Y)
        role_copy(h).start()

    for h in range(H):
        gather_wait(2, h, delta_all, Y)
        swap_send(h)
        layer(2, h, X, lambda s: dot(cut(delta_all, s, hr)[...], w2[...], 1, 1))

    def g_copy(which, out, into, block):
        return pltpu.make_async_remote_copy(
            src_ref=cut(out, block * wr, wr),
            dst_ref=into.at[z],
            send_sem=g_sem.at[0, which, block],
            recv_sem=g_sem.at[1, which, z],
            device_id=dev(at_z=block),
            device_id_type=MESH,
        )

    def g_term(which, left, right, out, into):
        for part in range(2):
            columns = pl.ds(part * half, half)
            for j in range(0, width, half):
                out[columns, pl.ds(j, half)] = dot(
                    left[:, columns], right[:, pl.ds(j, half)], 0, 0
                ).astype(BF16)

            def one(k, part=part):
                block = part * (nz // 2) + lax.rem(z + k, nz // 2)

                @pl.when(block != z)
                def _():
                    g_copy(which, out, into, block).start()

            each(0, nz // 2, one)
        into[z] = out[pl.ds(pl.multiple_of(z * wr, 16), wr), :]

    g_term(1, second_all, delta_all, g2_out, g2_in)

    for h in range(H):
        role_copy(h).wait_recv()
        for i in range(0, hr, max(STEP, gr)):
            count = max(STEP, gr)
            lev = wide(level[pl.ds(pl.multiple_of(row0(h, y) + i, 16), count), :])
            mine = pred[h, pl.ds(i, count), :].astype(F32)
            theirs = pred_other[h, pl.ds(i, count), :].astype(F32)
            diff = jnp.where(r == 1, mine - theirs, theirs - mine)
            diff = ((1.0 - lev) * diff).astype(BF16)
            some = pl.ds((h * hr + i) // gr, count // gr)
            for c in range(2):
                gap[c, some] = diff[:, c * half : (c + 1) * half].reshape(count // gr, gr, half)

    def back_copy(k):
        index = lax.rem(my_yz + k, groups)
        ay, az = yz(index)
        return remote(
            gap.at[r, index], back_in.at[my_yz], all_sem, (1, k), dev(at_y=ay, at_z=az)
        )

    each(1, groups, lambda k: back_copy(k).start())
    back_in[my_yz] = gap[r, my_yz]

    def norm_parts(h, i):
        at_rows = pl.ds(pl.multiple_of(row0(h, x) + i, 16), STEP)
        scale = 1.0 + wide(level[at_rows, :]) * mod_two[...]
        root = wide(root_p[at_rows, :])
        normed = hidden_all[at_rows, :].astype(F32) * root
        shaped = normed * scale
        sig = sigmoid(shaped)
        grad = layer_sum(2, h, i) * (sig * (1.0 + shaped * (1.0 - sig))) * scale
        return root, normed, grad

    def inner_copy(h, k):
        to = lax.rem(y + k, n)
        return remote(inner_out.at[h], inner_in.at[h, y], inner_sem, (h, k), dev(at_y=to))

    for h in range(H):
        layer_wait(2, h)
        for i in range(0, hr, STEP):
            _, normed, grad = norm_parts(h, i)
            own[0, h, pl.ds(i, STEP), :] = grad
            sums(i, grad * normed)
        inner_out[h] = column[...].T[0:8, :]
        inner_in[h, y] = inner_out[h]
        for k in range(1, n):
            inner_copy(h, k).start()

    for h in range(H):
        for k in range(1, n):
            piece = inner_in.at[h, lax.rem(y + n - k, n)]
            remote(piece, piece, inner_sem, (h, k), dev()).wait_recv()
        total = inner_in[h, 0]
        for c in range(1, n):
            total = total + inner_in[h, c]
        column[...] = jnp.broadcast_to(total[0:1, :] / D, (128, hr)).T
        swap_wait(h)
        for i in range(0, hr, STEP):
            at_rows = pl.ds(pl.multiple_of(row0(h, x) + i, 16), STEP)
            root = wide(root_p[at_rows, :])
            normed = hidden_all[at_rows, :].astype(F32) * root
            grad = own[0, h, pl.ds(i, STEP), :]
            back = root * (grad - normed * wide(column[pl.ds(i, STEP), :]))
            value = swap_buf[h, pl.ds(i, STEP), :].astype(F32) + back
            up_all[at_rows, :] = value.astype(BF16)
        gather_send(3, h, up_all, X)

    def back_wait(k):
        piece = back_in.at[lax.rem(my_yz + groups - k, groups)]
        remote(piece, piece, all_sem, (1, k), dev()).wait_recv()

    each(1, groups, back_wait)
    slots = back_in[...].reshape(rows, half)
    returned[r] = dot(place_back[...], slots, 1, 0).astype(BF16)
    ret_role = remote(returned.at[r], returned.at[r], one_sem, (4,), other)
    ret_role.start()
    ret_swap_copy = remote(returned.at[r], ret_swap, one_sem, (5,), across)
    swapping(ret_swap_copy, returned.at[r], ret_swap)
    theirs = returned.at[1 - r]
    remote(theirs, theirs, one_sem, (4,), other).wait_recv()
    ret_all[y] = returned[...]

    def ret_copy(k):
        return remote(returned, ret_all.at[y], gen_sem, (2, k), dev(at_y=lax.rem(y + k, n)))

    for k in range(1, n):
        ret_copy(k).start()

    for h in range(H):
        gather_wait(3, h, up_all, X)
    g_term(0, first_all, up_all, g1_out, g1_in)

    def g_finish(which, into, result):
        def wait(source):
            @pl.when(source != z)
            def _():
                piece = into.at[source]
                pltpu.make_async_remote_copy(
                    src_ref=piece,
                    dst_ref=piece,
                    send_sem=g_sem.at[0, which, source],
                    recv_sem=g_sem.at[1, which, source],
                    device_id=dev(),
                    device_id_type=MESH,
                ).wait_recv()

        each(0, nz, wait)
        for i in range(0, wr, STEP):
            total = into[0, pl.ds(i, STEP), :].astype(F32)
            for s in range(1, nz):
                total = total + into[s, pl.ds(i, STEP), :].astype(F32)
            result[pl.ds(i, STEP), :] = total.astype(result.dtype)

    g_finish(1, g2_in, g2_mine)
    g2_swap_copy = remote(g2_mine, g2_swap, one_sem, (6,), across)
    swapping(g2_swap_copy, g2_mine, g2_swap)

    for k in range(1, n):
        piece = ret_all.at[lax.rem(y + n - k, n)]
        remote(piece, piece, gen_sem, (2, k), dev()).wait_recv()

    def back_part_copy(k):
        to = dev(at_x=lax.rem(x + k, n))
        return remote(back_out.at[k], back_parts.at[k], gen_sem, (3, k), to)

    def back_part(k):
        part = lax.rem(x + k, n)
        total = dot(ret_all[part, 0], weight_half(0), 1, 1)
        total = total + dot(ret_all[part, 1], weight_half(1), 1, 1)
        return total

    def weight_half(c):
        return wg[pl.ds(pl.multiple_of(r * half, 16), half), pl.ds(c * half, half)]

    def back_send(k):
        back_out[k] = back_part(k).astype(BF16)
        back_part_copy(k).start()

    each(1, n, back_send)
    back_own[...] = back_part(0)
    for k in range(1, n):
        back_part_copy(k).wait_recv()

    def my_half(ref, at_rows):
        low, high = ref[at_rows, pl.ds(0, half)], ref[at_rows, pl.ds(half, half)]
        return jnp.where(r == 1, high.astype(F32), low.astype(F32))

    def narrow(value):
        return jnp.concatenate([value] * (half // 128), axis=1)

    def gen_normed(i):
        at_rows = pl.ds(i, STEP)
        root = narrow(root_g[pl.ds(pl.multiple_of(x * toks + i, 16), STEP), :])
        return root, my_half(noise, at_rows) * root

    gain_half = my_half(gain, pl.ds(0, 1))
    for i in range(0, toks, STEP):
        at_rows = pl.ds(i, STEP)
        _, normed = gen_normed(i)
        shaped = normed * gain_half
        sig = sigmoid(shaped)
        total = back_own[at_rows, :]
        for k in range(1, n):
            total = total + back_parts[k, at_rows, :].astype(F32)
        grad = total * (sig * (1.0 + shaped * (1.0 - sig))) * gain_half
        back_own[at_rows, :] = grad
        sums(i, grad * normed)
    summed = column[...].T[0:8, :]
    gen_inner_out[...] = summed
    spot = r * n + y
    gen_inner_in[spot] = summed

    def gen_inner_copy(k):
        index = lax.rem(spot + k, 2 * n)
        to = dev(role=index // n, at_y=lax.rem(index, n))
        return remote(gen_inner_out, gen_inner_in.at[spot], gen_inner_sem, (k,), to)

    for k in range(1, 2 * n):
        gen_inner_copy(k).start()
    for k in range(1, 2 * n):
        piece = gen_inner_in.at[lax.rem(spot + 2 * n - k, 2 * n)]
        remote(piece, piece, gen_inner_sem, (k,), dev()).wait_recv()
    total = gen_inner_in[0]
    for c in range(1, 2 * n):
        total = total + gen_inner_in[c]
    column[...] = jnp.broadcast_to(total[0:1, :] / D, (128, toks)).T
    arrived(ret_swap_copy)
    for i in range(0, toks, STEP):
        at_rows = pl.ds(i, STEP)
        root, normed = gen_normed(i)
        back = root * (back_own[at_rows, :] - normed * narrow(column[at_rows, :]))
        noise_grad[at_rows, :] = ret_swap[at_rows, :].astype(F32) + back

    g_finish(0, g1_in, grad_one)
    arrived(g2_swap_copy)
    grad_two[...] = g2_swap[...].astype(F32)

    def g_sent(which, out, into):
        def done(block):
            @pl.when(block != z)
            def _():
                g_copy(which, out, into, block).wait_send()

        each(0, nz, done)

    g_sent(1, g2_out, g2_in)
    g_sent(0, g1_out, g1_in)

    for copy in sent:
        copy.wait_send()
    each(1, nz, lambda k: w1_copy(k).wait_send())
    each(1, nz, lambda k: w2_copy(k).wait_send())

    each(1, nz, lambda k: wg_copy(k).wait_send())
    each(0, nz, lambda k: wg_role(k).wait_send())
    each(1, groups, lambda k: clean_copy(k).wait_send())
    each(1, groups, lambda k: back_copy(k).wait_send())
    clean_role.wait_send()
    cnoise_role.wait_send()
    ret_role.wait_send()
    each(1, group, lambda k: remote(
        stat_out.at[2, 0], stat_out.at[2, 0], stat_sem, (2, 0, k), dev()
    ).wait_send())

    @pl.when(x != y)
    def _():
        wg_copy(None).wait_send()
        for copy in (noise_swap_copy, w2_swap, cnoise_swap, ret_swap_copy, g2_swap_copy):
            copy.wait_send()

    for k in range(1, n):
        for copy in (noise_copy, level_copy, gen_copy, ret_copy, back_part_copy):
            copy(k).wait_send()
    for k in range(1, 2 * n):
        gen_inner_copy(k).wait_send()

    for h in range(H):
        role_copy(h).wait_send()
        for k in range(1, n):
            noisy_copy(h, k).wait_send()
            noisy_role(h, k).wait_send()
        swap_sent(h)
        for phase in range(3):
            def part_sent(k, phase=phase, h=h):
                piece = part_in.at[phase, h, k]
                remote(piece, piece, rs_sem, (phase, h, k), dev()).wait_send()

            each(1, n, part_sent)
        for phase in range(2):

            def stat_sent(k, phase=phase, h=h):
                piece = stat_out.at[phase, h]
                remote(piece, piece, stat_sem, (phase, h, k), dev()).wait_send()

            each(1, group, stat_sent)
        for k in range(1, n):
            inner_copy(h, k).wait_send()


def step(n, nz, *operands):
    noise, cnoise, w1_shard = operands[0], operands[5], operands[9]
    toks, width = noise.shape
    rows = cnoise.shape[0]
    hr, th, half = rows // H, toks // 2, width // 2
    wr = w1_shard.shape[0]
    group, groups = n * n, n * nz
    gr = rows // groups
    vmem = pl.BlockSpec(memory_space=pltpu.VMEM)
    bf = lambda *shape: pltpu.VMEM(shape, BF16)
    fl = lambda *shape: pltpu.VMEM(shape, F32)
    sems = lambda *shape: pltpu.SemaphoreType.DMA((2, *shape))
    whole = bf(n * rows, width)
    square = bf(nz * wr, width)
    pieces = bf(nz, wr, width)
    return pl.pallas_call(
        functools.partial(step_kernel, n, nz),
        out_shape=(
            jax.ShapeDtypeStruct((toks, half), F32),
            jax.ShapeDtypeStruct((wr, width), F32),
            jax.ShapeDtypeStruct((wr, width), F32),
        ),
        in_specs=[vmem] * 11,
        out_specs=(vmem,) * 3,
        scratch_shapes=[
            square,
            square,
            *[whole] * 6,
            fl(n * rows, 128),
            fl(n * rows, 128),
            fl(n * rows, 128),
            bf(rows, width),
            bf(rows, width),
            bf(H, hr, width),
            bf(H, hr, width),
            bf(H, hr, width),
            bf(3, n * rows, width),
            bf(3, H, n, hr, width),
            fl(3, H, hr, width),
            square,
            pieces,
            square,
            pieces,
            fl(hr, 128),
            fl(3, H, 8, hr),
            fl(3, H, group, 8, hr),
            fl(H, 8, hr),
            fl(H, n, 8, hr),
            fl(n, H, 8, hr),
            square,
            bf(wr, width),
            bf(n, th, width),
            bf(th, width),
            bf(n, th, width),
            fl(n * toks, 128),
            bf(th, width),
            bf(n, th, width),
            bf(n, th, width),
            fl(th, width),
            bf(groups, gr, width),
            bf(groups, gr, width),
            bf(groups, gr, width),
            bf(2, groups, gr, half),
            bf(groups, gr, half),
            bf(2, toks, half),
            bf(n, 2, toks, half),
            bf(toks, half),
            bf(n, toks, half),
            bf(n, toks, half),
            fl(toks, half),
            fl(8, toks),
            fl(2 * n, 8, toks),
            bf(wr, width),
            bf(wr, width),
            sems(2, nz),
            sems(4, H, n),
            sems(3, H, n),
            sems(H),
            sems(3, H, group),
            sems(H, n),
            sems(2, nz),
            sems(H),
            sems(n),
            sems(nz),
            sems(nz),
            sems(8),
            sems(4, n),
            sems(2, groups),
            sems(H, n),
            sems(2 * n),
        ],
        compiler_params=pltpu.CompilerParams(
            collective_id=0, has_side_effects=True, vmem_limit_bytes=62 * 2**20
        ),
    )(*operands)


def shards(
    noise,
    gen_gain,
    gen_weight,
    routes,
    critic_noise,
    critic_steps,
    crit_mod,
    crit_first,
    crit_second,
):
    width = noise.shape[1]
    groups = lax.axis_size(DP)
    x, y, z, role = (lax.axis_index(a) for a in (X, Y, Z, R))
    blocks_here = noise.shape[0] // BT
    most = 2 * blocks_here // groups

    rows = critic_noise.shape[0]
    level = jnp.repeat(critic_steps.astype(F32) / levels, BT).reshape(H, 1, rows // H)
    level = jnp.broadcast_to(level, (H, 8, rows // H))

    me_index = y * lax.axis_size(Z) + z
    table = routes[:, 0]
    target_index = lax.dynamic_slice_in_dim(table, me_index * blocks_here, blocks_here, 0)
    order = jnp.arange(blocks_here, dtype=jnp.int32)
    earlier = (target_index[:, None] == target_index[None, :]) & (order[None, :] < order[:, None])
    rank = jnp.sum(earlier.astype(jnp.int32), axis=1)
    first_row = (target_index * most + rank) * BT
    row_of_token = (first_row[:, None] + jnp.arange(BT, dtype=jnp.int32)).reshape(-1)
    place_back = (row_of_token[:, None] == jnp.arange(rows, dtype=jnp.int32)[None, :]).astype(BF16)
    mine = row_of_token.reshape(2, -1)
    mine = jnp.where(role == 1, mine[1], mine[0])
    place = (jnp.arange(rows, dtype=jnp.int32)[:, None] == mine[None, :]).astype(BF16)
    counts = jnp.sum((table.reshape(groups, blocks_here) == me_index).astype(jnp.int32), axis=1)
    filled = (jnp.arange(most, dtype=jnp.int32)[None, :] < counts[:, None]).astype(F32)
    valid = jnp.repeat(filled.reshape(groups * most), BT)[:, None] / TOK_DEV

    noise_grad, grad_one, grad_two = step(
        lax.axis_size(X),
        lax.axis_size(Z),
        noise,
        gen_gain[None, :],
        gen_weight,
        place,
        place_back,
        critic_noise,
        level,
        jnp.broadcast_to(valid, (rows, 128)),
        crit_mod[0],
        crit_first[0],
        crit_second[0],
    )
    return (noise_grad.reshape(-1, 1, 1, width // 2), grad_one[None], grad_two[None])


def solution(mesh):
    split = Mesh(
        mesh.devices.reshape(mesh.shape[R], mesh.shape[Y], -1, mesh.shape[Y]),
        (R, X, Z, Y),
    )
    in_specs = (
        P(DP, Y),
        P(),
        P(DP, Y),
        P(),
        P(DP, Y),
        P(DP),
        P(R, None, None),
        P(R, DP, Y),
        P(R, DP, Y),
    )
    out_specs = (P(DP, Y, R, None), P(R, DP, Y), P(R, DP, Y))
    return jax.shard_map(
        shards, mesh=split, in_specs=in_specs, out_specs=out_specs, check_vma=False
    )
```
